512 devices in a mesh: section: 8 (over z_hi, x), rows: 64 (over z_lo, y, core).
Axes of the slice: x: 4, y: 8, z: 8 (z_hi: 2, z_lo: 4; z = z_hi * 4 + z_lo), core: 2. Of those that a mesh axis runs over, the one named last changes fastest.
Arguments:
- frames_in: bfloat16 [8, 2, 128, 64, 256], P(None, None, 'rows'), may hold values from -6 to 6
- layer_weights: bfloat16 [8, 2, 3, 3, 256, 256], P('section'), may hold values from -0.09375 to 0.09375
Outputs:
- layer_outputs: bfloat16 [8, 8, 2, 128, 64, 256], P('section', None, None, 'rows')
The draws below stay inside these ranges and needn't reach their ends.
All inputs are finite; a program needn't handle non-finite values.
Results may differ from the reference program's by a relative error of at most 0.009.
Values may be sent and summed in bfloat16 or wider, within the bound.
No kernel may reach another device: no remote copies, remote signals or barrier semaphores. Data moves between devices by JAX's collectives and lax.ppermute only.
A program may use at most 64 MiB of HBM per device.

```python
import jax
import jax.numpy as jnp
from jax import lax

C = 256
W = 64
F = 2
M = 8
LAYERS = 8
H = 128


def levels(rng, dims, cuts, smallest, largest):
    loudness, own = 1.0, jax.random.fold_in(rng, 6)
    for dim, parts in cuts:
        heights = jnp.exp(jax.random.uniform(jax.random.fold_in(own, dim), (parts,), jnp.float32, smallest / len(cuts), largest / len(cuts)))
        loudness = loudness * jnp.repeat(heights, dims[dim] // parts).reshape([-1 if axis == dim else 1 for axis in range(len(dims))])
    return loudness


def scatter_about(key, dims, scale, bound, split=(), kind=jnp.bfloat16):
    loudness = levels(key, dims, split, -0.22, 0.18) if split else 1.0
    array = jax.random.normal(key, dims, jnp.float32) * scale * loudness
    return jnp.minimum(jnp.maximum(array, -bound), bound).astype(kind)


def setup_inputs(seed: int = 0) -> dict:
    key_list = jax.random.split(jax.random.key(seed), 3)
    frames_in = scatter_about(key_list[0], (M, F, H, W, C), 1.0, 6.0, ((2, 64),))
    layer_weights = scatter_about(key_list[1], (LAYERS, 2, 3, 3, C, C), (18 * C) ** -0.5, 0.09375, ((0, 8),))
    return dict(frames_in=frames_in, layer_weights=layer_weights)


def normalize(clip):
    values = clip.astype(jnp.float32)
    scale = lax.rsqrt(lax.optimization_barrier(jnp.mean(values * values, axis=-1, keepdims=True)) + 1e-06)
    return (values * scale).astype(jnp.bfloat16)

def reference(frames_in, layer_weights):
    current = frames_in
    results = []
    for layer in range(LAYERS):
        kernel = layer_weights[layer].astype(jnp.float32)

        def one_clip(clip):
            normed = normalize(clip)
            padded = jnp.pad(normed, ((1, 0), (1, 1), (1, 1), (0, 0))).astype(jnp.float32)
            conv = lax.conv_general_dilated(padded[None], kernel, (1, 1, 1), 'VALID', dimension_numbers=('NDHWC', 'DHWIO', 'NDHWC'))[0]
            return (clip.astype(jnp.float32) + jax.nn.silu(conv)).astype(jnp.bfloat16)
        current = lax.map(one_clip, current)
        results.append(current)
    return jnp.stack(results)
```

```python
import jax
import jax.numpy as jnp
from jax import lax
from jax.experimental import pallas as pl
from jax.experimental.pallas import tpu as pltpu
from jax.sharding import PartitionSpec as P

DEPTH = 4
CHUNK = 2


def stage_kernel(meta, top, mid, bot, own, left_mine, left_theirs, right_mine, right_theirs, far_mine, far_theirs,
                 kept, last, weights, cells, wide, sems):
    x, core, chip, piece, chips = meta[0], meta[1], meta[2], meta[3], meta[4]
    depth, _, taps, chans = weights.shape
    frames, slab, width, _ = mid.shape
    rows = 3 * slab
    part = taps // 4
    other = 1 - core

    def copy(src, dst, sem):
        pltpu.make_async_copy(src, dst, sem).start()

    for layer in range(depth):
        step = lax.rem(layer - x + depth, depth)
        sem = sems.at[layer]

        @pl.when(step == 0)
        def _():
            copy(own, weights.at[layer], sem)

        @pl.when(step == 1)
        def _():
            copy(right_mine, weights.at[layer, core], sem)
            copy(right_theirs, weights.at[layer, other], sem)

        @pl.when(step == 3)
        def _():
            copy(left_mine, weights.at[layer, core], sem)
            copy(left_theirs, weights.at[layer, other], sem)

        @pl.when(step == 2)
        def _():
            for place, shift in enumerate((0, 3, 1, 2)):
                at = pl.ds(pl.multiple_of(lax.rem(piece + shift, 4) * part, part), part)
                copy(far_mine.at[place], weights.at[layer, core, at], sem)
                copy(far_theirs.at[place], weights.at[layer, other, at], sem)

    cells[:, 0:slab] = top[...]
    cells[:, slab:2 * slab] = mid[...]
    cells[:, 2 * slab:] = bot[...]
    column = lax.broadcasted_iota(jnp.int32, (width, chans), 0)

    for layer in range(depth):
        def normalize(row, carry):
            place = chip * slab - slab + row
            inside = jnp.logical_and(place >= 0, place < chips * slab)
            for frame in range(frames):
                values = cells[frame, row].astype(jnp.float32)
                scale = lax.rsqrt(jnp.mean(values * values, axis=-1, keepdims=True) + 1e-06)
                normed = jnp.where(inside, values * scale, 0.0)
                before = jnp.where(column == 0, 0.0, pltpu.roll(normed, 1, 0))
                after = jnp.where(column == width - 1, 0.0, pltpu.roll(normed, width - 1, 0))
                wide[frame, row, :, 0:chans] = before.astype(jnp.bfloat16)
                wide[frame, row, :, chans:2 * chans] = normed.astype(jnp.bfloat16)
                wide[frame, row, :, 2 * chans:] = after.astype(jnp.bfloat16)
            return carry

        lax.fori_loop(layer, rows - layer, normalize, 0)
        pltpu.make_async_copy(own, weights.at[layer], sems.at[layer]).wait()

        def convolve(index, carry):
            row = layer + 1 + index * CHUNK
            size = CHUNK * width
            total = jnp.zeros((frames * size, chans), jnp.float32)
            older = jnp.zeros((size, chans), jnp.float32)
            for tap in range(3):
                at = pl.ds(tap * 3 * chans, 3 * chans)
                both = wide[:, pl.ds(row - 1 + tap, CHUNK)].reshape(frames * size, 3 * chans)
                total += jnp.dot(both, weights[layer, 1, at], preferred_element_type=jnp.float32)
                older += jnp.dot(both[:size], weights[layer, 0, at], preferred_element_type=jnp.float32)
            for frame in range(frames):
                conv = total[frame * size:(frame + 1) * size]
                if frame:
                    conv = conv + older
                conv = conv.reshape(CHUNK, width, chans)
                values = cells[frame, pl.ds(row, CHUNK)].astype(jnp.float32)
                cells[frame, pl.ds(row, CHUNK)] = (values + conv / (1.0 + jnp.exp(-conv))).astype(jnp.bfloat16)
            return carry

        lax.fori_loop(0, (rows - 2 * layer - 2) // CHUNK, convolve, 0)
        half = slab // 2
        kept[core, layer] = cells[:, slab:slab + half]
        kept[other, layer] = cells[:, slab + half:2 * slab]
    last[...] = cells[:, slab:2 * slab]


def run_stage(meta, top, mid, bot, kernels):
    frames, slab, width, chans = mid.shape
    taps = kernels[0].shape[1]
    vmem = pl.BlockSpec(memory_space=pltpu.VMEM)
    hbm = pl.BlockSpec(memory_space=pl.ANY)
    bf16 = jnp.bfloat16
    return pl.pallas_call(
        stage_kernel,
        out_shape=(
            jax.ShapeDtypeStruct((2, DEPTH, frames, slab // 2, width, chans), bf16),
            jax.ShapeDtypeStruct((frames, slab, width, chans), bf16),
        ),
        in_specs=[pl.BlockSpec(memory_space=pltpu.SMEM)] + [vmem] * 3 + [hbm] * len(kernels),
        out_specs=(vmem, vmem),
        scratch_shapes=[
            pltpu.VMEM((DEPTH, 2, taps, chans), bf16),
            pltpu.VMEM((frames, 3 * slab, width, chans), bf16),
            pltpu.VMEM((frames, 3 * slab, width, 3 * chans), bf16),
            pltpu.SemaphoreType.DMA((DEPTH,)),
        ],
        compiler_params=pltpu.CompilerParams(vmem_limit_bytes=40 * 1024 * 1024),
        cost_estimate=pl.CostEstimate(flops=7 * 10**9, bytes_accessed=12 * 10**6, transcendentals=10**6),
        name="stage",
    )(meta, top, mid, bot, *kernels)


def place_kernel(meta, *refs):
    sources, out, sems = refs[:-2], refs[-2], refs[-1]
    x, core = meta[0], meta[1]
    copies = []
    for shift in range(4):
        group = lax.rem(x - shift + 4, 4)
        for which in range(2):
            clip = 2 * group + (core if which == 0 else 1 - core)
            source = sources[2 * shift + which]
            copies.append(pltpu.make_async_copy(source, out.at[clip], sems.at[2 * shift + which]))
    for one in copies:
        one.start()
    for one in copies:
        one.wait()


def place(meta, sources):
    shape = sources[0].shape
    hbm = pl.BlockSpec(memory_space=pl.ANY)
    return pl.pallas_call(
        place_kernel,
        out_shape=jax.ShapeDtypeStruct((8,) + shape, jnp.bfloat16),
        in_specs=[pl.BlockSpec(memory_space=pltpu.SMEM)] + [hbm] * 8,
        out_specs=hbm,
        scratch_shapes=[pltpu.SemaphoreType.DMA((8,))],
        name="place",
    )(meta, *sources)


def route(move, keep=lambda zh, x, zl, y, c: True):
    pairs = []
    for zh in range(2):
        for x in range(4):
            for zl in range(4):
                for y in range(8):
                    for c in range(2):
                        here = (zh, x, zl, y, c)
                        there = move(*here)
                        if there is not None and keep(*here):
                            pairs.append(tuple((((d[0] * 4 + d[1]) * 4 + d[2]) * 8 + d[3]) * 2 + d[4] for d in (here, there)))
    return pairs


def next_chip(step):
    def move(zh, x, zl, y, c):
        chip = zl * 8 + y + step
        return (zh, x, chip // 8, chip % 8, c) if 0 <= chip < 32 else None
    return move


def send(array, move, keep=lambda *here: True):
    return lax.ppermute(array, ("section", "rows"), route(move, keep))


def along_x(step):
    return lambda zh, x, zl, y, c: (zh, (x + step) % 4, zl, y, c)


def along_y(step):
    return lambda zh, x, zl, y, c: (zh, x, zl, (y + step) % 8, c)


def sibling(zh, x, zl, y, c):
    return (zh, x, zl, y, 1 - c)


def local(frames_in, layer_weights):
    section, row = lax.axis_index("section"), lax.axis_index("rows")
    x, upper = section % 4, section // 4
    core, chip = row % 2, row // 2
    piece = chip % 4
    meta = jnp.stack([x, core, chip, piece, jnp.int32(32)]).astype(jnp.int32)
    chans = frames_in.shape[-1]

    own = layer_weights.reshape(2, 9 * chans, chans)
    mine = lax.dynamic_index_in_dim(own, core, 0, keepdims=False)
    part = mine.shape[0] // 4
    quarter = lax.dynamic_slice_in_dim(mine, piece * part, part, 0)

    far = send(quarter, along_x(2))
    left_mine = send(mine, along_x(1))
    right_mine = send(mine, along_x(-1))

    give = lax.dynamic_index_in_dim(frames_in, 2 * x + 1 - core, 0, keepdims=False)
    keep = lax.dynamic_index_in_dim(frames_in, 2 * x + core, 0, keepdims=False)
    got = send(give, sibling)
    mid = jnp.where(core == 0, jnp.concatenate([keep, got], 1), jnp.concatenate([got, keep], 1))
    top = send(mid, next_chip(1))
    bot = send(mid, next_chip(-1))

    far_mine = jnp.stack([far, send(far, along_y(1)), send(far, along_y(-1)), send(far, along_y(2))])
    far_theirs = send(far_mine, sibling)
    left_theirs = send(left_mine, sibling)
    right_theirs = send(right_mine, sibling)
    kernels = (own, left_mine, left_theirs, right_mine, right_theirs, far_mine, far_theirs)

    first, reached = run_stage(meta, top, mid, bot, kernels)

    mid = send(reached, lambda zh, x, zl, y, c: (1, x, zl, y, c), lambda zh, *_: zh == 0)
    top = send(mid, next_chip(1), lambda zh, *_: zh == 1)
    bot = send(mid, next_chip(-1), lambda zh, *_: zh == 1)
    second, _ = run_stage(meta, top, mid, bot, kernels)

    done = jnp.where(upper == 0, first, second)
    theirs = send(done[1], sibling)
    both = (done[0], theirs)
    sources = [lax.dynamic_index_in_dim(one, x, 0, keepdims=False) for one in both]
    for step in (1, 2, 3):
        layer = (x + step) % 4
        pair = jnp.stack([lax.dynamic_index_in_dim(one, layer, 0, keepdims=False) for one in both])
        got = send(pair, along_x(step))
        sources += [got[0], got[1]]
    return place(meta, sources)[None]


def solution(mesh):
    placed = (P(None, None, "rows", None, None), P("section", None, None, None, None, None))
    return jax.shard_map(
        local,
        mesh=mesh,
        in_specs=placed,
        out_specs=P("section", None, None, "rows", None, None),
        check_vma=False,
    )
```

```python
import jax
import jax.numpy as jnp
from jax import lax
from jax.experimental import pallas as pl
from jax.experimental.pallas import tpu as pltpu
from jax.sharding import PartitionSpec as P

DEPTH = 4
CHUNK = 2


def stage_kernel(meta, top, mid, bot, own_mine, own_theirs, left_mine, left_theirs, right_mine, right_theirs, far_mine, far_theirs,
                 kept, last, weights, cells, wide, sems):
    x, core, chip, piece, chips = meta[0], meta[1], meta[2], meta[3], meta[4]
    depth, _, taps, chans = weights.shape
    frames, slab, width, _ = mid.shape
    rows = 3 * slab
    part = taps // 4
    other = 1 - core

    def copy(src, dst, sem):
        pltpu.make_async_copy(src, dst, sem).start()

    for layer in range(depth):
        step = lax.rem(layer - x + depth, depth)
        sem = sems.at[layer]

        @pl.when(step == 0)
        def _():
            copy(own_mine, weights.at[layer, core], sem)
            copy(own_theirs, weights.at[layer, other], sem)

        @pl.when(step == 1)
        def _():
            copy(right_mine, weights.at[layer, core], sem)
            copy(right_theirs, weights.at[layer, other], sem)

        @pl.when(step == 3)
        def _():
            copy(left_mine, weights.at[layer, core], sem)
            copy(left_theirs, weights.at[layer, other], sem)

        @pl.when(step == 2)
        def _():
            for place, shift in enumerate((0, 3, 1, 2)):
                at = pl.ds(pl.multiple_of(lax.rem(piece + shift, 4) * part, part), part)
                copy(far_mine.at[place], weights.at[layer, core, at], sem)
                copy(far_theirs.at[place], weights.at[layer, other, at], sem)

    cells[:, 0:slab] = top[...]
    cells[:, slab:2 * slab] = mid[...]
    cells[:, 2 * slab:] = bot[...]
    column = lax.broadcasted_iota(jnp.int32, (width, chans), 0)

    for layer in range(depth):
        def normalize(row, carry):
            place = chip * slab - slab + row
            inside = jnp.logical_and(place >= 0, place < chips * slab)
            for frame in range(frames):
                values = cells[frame, row].astype(jnp.float32)
                scale = lax.rsqrt(jnp.mean(values * values, axis=-1, keepdims=True) + 1e-06)
                normed = jnp.where(inside, values * scale, 0.0)
                before = jnp.where(column == 0, 0.0, pltpu.roll(normed, 1, 0))
                after = jnp.where(column == width - 1, 0.0, pltpu.roll(normed, width - 1, 0))
                wide[frame, row, :, 0:chans] = before.astype(jnp.bfloat16)
                wide[frame, row, :, chans:2 * chans] = normed.astype(jnp.bfloat16)
                wide[frame, row, :, 2 * chans:] = after.astype(jnp.bfloat16)
            return carry

        lax.fori_loop(layer, rows - layer, normalize, 0)
        pltpu.make_async_copy(weights.at[layer], weights.at[layer], sems.at[layer]).wait()

        def convolve(index, carry):
            row = layer + 1 + index * CHUNK
            size = CHUNK * width
            total = jnp.zeros((frames * size, chans), jnp.float32)
            older = jnp.zeros((size, chans), jnp.float32)
            for tap in range(3):
                at = pl.ds(tap * 3 * chans, 3 * chans)
                both = wide[:, pl.ds(row - 1 + tap, CHUNK)].reshape(frames * size, 3 * chans)
                total += jnp.dot(both, weights[layer, 1, at], preferred_element_type=jnp.float32)
                older += jnp.dot(both[:size], weights[layer, 0, at], preferred_element_type=jnp.float32)
            for frame in range(frames):
                conv = total[frame * size:(frame + 1) * size]
                if frame:
                    conv = conv + older
                conv = conv.reshape(CHUNK, width, chans)
                values = cells[frame, pl.ds(row, CHUNK)].astype(jnp.float32)
                cells[frame, pl.ds(row, CHUNK)] = (values + conv / (1.0 + jnp.exp(-conv))).astype(jnp.bfloat16)
            return carry

        lax.fori_loop(0, (rows - 2 * layer - 2) // CHUNK, convolve, 0)
        half = slab // 2
        kept[core, layer] = cells[:, slab:slab + half]
        kept[other, layer] = cells[:, slab + half:2 * slab]
    last[...] = cells[:, slab:2 * slab]


def run_stage(meta, top, mid, bot, kernels):
    frames, slab, width, chans = mid.shape
    taps = kernels[0].shape[0]
    vmem = pl.BlockSpec(memory_space=pltpu.VMEM)
    hbm = pl.BlockSpec(memory_space=pl.ANY)
    bf16 = jnp.bfloat16
    return pl.pallas_call(
        stage_kernel,
        out_shape=(
            jax.ShapeDtypeStruct((2, DEPTH, frames, slab // 2, width, chans), bf16),
            jax.ShapeDtypeStruct((frames, slab, width, chans), bf16),
        ),
        in_specs=[pl.BlockSpec(memory_space=pltpu.SMEM)] + [vmem] * 3 + [hbm] * len(kernels),
        out_specs=(vmem, vmem),
        scratch_shapes=[
            pltpu.VMEM((DEPTH, 2, taps, chans), bf16),
            pltpu.VMEM((frames, 3 * slab, width, chans), bf16),
            pltpu.VMEM((frames, 3 * slab, width, 3 * chans), bf16),
            pltpu.SemaphoreType.DMA((DEPTH,)),
        ],
        compiler_params=pltpu.CompilerParams(vmem_limit_bytes=40 * 1024 * 1024),
        cost_estimate=pl.CostEstimate(flops=7 * 10**9, bytes_accessed=12 * 10**6, transcendentals=10**6),
        name="stage",
    )(meta, top, mid, bot, *kernels)


def place_kernel(meta, home, away, *refs):
    arrived, out = refs[:-1], refs[-1]
    x, core = meta[0], meta[1]
    out[2 * x + core] = home[...]
    out[2 * x + 1 - core] = away[...]
    for shift, pair in enumerate(arrived, 1):
        group = lax.rem(x - shift + 4, 4)
        out[2 * group + core] = pair[0]
        out[2 * group + 1 - core] = pair[1]


def place(meta, home, away, arrived):
    vmem = pl.BlockSpec(memory_space=pltpu.VMEM)
    return pl.pallas_call(
        place_kernel,
        out_shape=jax.ShapeDtypeStruct((8,) + home.shape, jnp.bfloat16),
        in_specs=[pl.BlockSpec(memory_space=pltpu.SMEM)] + [vmem] * (2 + len(arrived)),
        out_specs=vmem,
        compiler_params=pltpu.CompilerParams(vmem_limit_bytes=8 * 1024 * 1024),
        name="place",
    )(meta, home, away, *arrived)


def route(move, keep=lambda zh, x, zl, y, c: True):
    pairs = []
    for zh in range(2):
        for x in range(4):
            for zl in range(4):
                for y in range(8):
                    for c in range(2):
                        here = (zh, x, zl, y, c)
                        there = move(*here)
                        if there is not None and keep(*here):
                            pairs.append(tuple((((d[0] * 4 + d[1]) * 4 + d[2]) * 8 + d[3]) * 2 + d[4] for d in (here, there)))
    return pairs


def next_chip(step):
    def move(zh, x, zl, y, c):
        chip = zl * 8 + y + step
        return (zh, x, chip // 8, chip % 8, c) if 0 <= chip < 32 else None
    return move


def send(array, move, keep=lambda *here: True):
    return lax.ppermute(array, ("section", "rows"), route(move, keep))


def along_x(step):
    return lambda zh, x, zl, y, c: (zh, (x + step) % 4, zl, y, c)


def along_y(step):
    return lambda zh, x, zl, y, c: (zh, x, zl, (y + step) % 8, c)


def sibling(zh, x, zl, y, c):
    return (zh, x, zl, y, 1 - c)


def local(frames_in, layer_weights):
    section, row = lax.axis_index("section"), lax.axis_index("rows")
    x, upper = section % 4, section // 4
    core, chip = row % 2, row // 2
    piece = chip % 4
    meta = jnp.stack([x, core, chip, piece, jnp.int32(32)]).astype(jnp.int32)
    chans = frames_in.shape[-1]

    own = layer_weights.reshape(2, 9 * chans, chans)
    part = own.shape[1] // 4
    quarter = lax.dynamic_slice(own, (core, piece * part, 0), (1, part, chans))[0]
    far = send(quarter, along_x(2))

    give = lax.dynamic_index_in_dim(frames_in, 2 * x + 1 - core, 0, keepdims=False)
    keep = lax.dynamic_index_in_dim(frames_in, 2 * x + core, 0, keepdims=False)
    got = send(give, sibling)
    mine = lax.dynamic_index_in_dim(own, core, 0, keepdims=False)
    theirs = lax.dynamic_index_in_dim(own, 1 - core, 0, keepdims=False)
    far, mine, got = lax.optimization_barrier((far, mine, got))
    left_mine = send(mine, along_x(1))
    right_mine = send(mine, along_x(-1))
    mid = jnp.where(core == 0, jnp.concatenate([keep, got], 1), jnp.concatenate([got, keep], 1))
    top = send(mid, next_chip(1))
    bot = send(mid, next_chip(-1))

    far, top, bot = lax.optimization_barrier((far, top, bot))
    far_mine = jnp.stack([far, send(far, along_y(1)), send(far, along_y(-1)), send(far, along_y(2))])
    far_theirs = send(far_mine, sibling)
    left_theirs = send(left_mine, sibling)
    right_theirs = send(right_mine, sibling)
    kernels = (mine, theirs, left_mine, left_theirs, right_mine, right_theirs, far_mine, far_theirs)

    first, reached = run_stage(meta, top, mid, bot, kernels)

    mid = send(reached, lambda zh, x, zl, y, c: (1, x, zl, y, c), lambda zh, *_: zh == 0)
    top = send(mid, next_chip(1), lambda zh, *_: zh == 1)
    bot = send(mid, next_chip(-1), lambda zh, *_: zh == 1)
    second, _ = run_stage(meta, top, mid, bot, kernels)

    done = jnp.where(upper == 0, first, second)
    both = (done[0], send(done[1], sibling))
    home, away = [lax.dynamic_index_in_dim(one, x, 0, keepdims=False) for one in both]
    arrived = []
    for step in (1, 2, 3):
        layer = (x + step) % 4
        pair = jnp.stack([lax.dynamic_index_in_dim(one, layer, 0, keepdims=False) for one in both])
        arrived.append(send(pair, along_x(step)))
    return place(meta, home, away, arrived)[None]


def solution(mesh):
    placed = (P(None, None, "rows", None, None), P("section", None, None, None, None, None))
    return jax.shard_map(
        local,
        mesh=mesh,
        in_specs=placed,
        out_specs=P("section", None, None, "rows", None, None),
        check_vma=False,
    )
```

```python
import functools

import jax
import jax.numpy as jnp
from jax import lax
from jax.experimental import pallas as pl
from jax.experimental.pallas import tpu as pltpu
from jax.sharding import PartitionSpec as P

DEPTH = 4
SPLIT = 4


def frame_kernel(frame, meta, top, mid, bot, *refs):
    first = frame == 0
    refs = list(refs)
    pieces = refs[:8]
    older = refs[8]
    kept, last = (refs[9], refs[10]) if not first else (refs[8], refs[9])
    older = refs[8] if not first else refs[10]
    weights, cells, wide, sems = refs[11:]
    x, core, chip, piece, chips = meta[0], meta[1], meta[2], meta[3], meta[4]
    depth, _, taps, chans = weights.shape
    _, slab, width, _ = mid.shape
    rows = 3 * slab
    other = 1 - core
    used = (0, 1) if first else (1,)

    def fetch(layer, mine, theirs, places):
        for half in used:
            for source, owner in ((mine, core), (theirs, other)):
                @pl.when(owner == half)
                def _():
                    for at, block in places(source):
                        pltpu.make_async_copy(block, weights.at[layer, half, at], sems.at[layer]).start()

    def whole(source):
        return [(slice(None), source)]

    def quarters(source):
        part = taps // 4
        return [(pl.ds(pl.multiple_of(lax.rem(piece + shift, 4) * part, part), part), source.at[place])
                for place, shift in enumerate((0, 3, 1, 2))]

    for layer in range(depth):
        step = lax.rem(layer - x + depth, depth)
        for distance, at in ((0, 0), (1, 4), (3, 2), (2, 6)):
            @pl.when(step == distance)
            def _():
                fetch(layer, pieces[at], pieces[at + 1], quarters if distance == 2 else whole)

    column = lax.broadcasted_iota(jnp.int32, (width, chans), 0)

    def spread(row, stored, buffer):
        values = stored.astype(jnp.float32)
        place = chip * slab - slab + row
        inside = jnp.logical_and(place >= 0, place < chips * slab)
        scale = lax.rsqrt(jnp.mean(values * values, axis=-1, keepdims=True) + 1e-06)
        normed = values * jnp.where(inside, scale, 0.0)
        before = jnp.where(column == 0, 0.0, pltpu.roll(normed, 1, 0))
        after = jnp.where(column == width - 1, 0.0, pltpu.roll(normed, width - 1, 0))
        wide[buffer, row, :, 0:chans] = before.astype(jnp.bfloat16)
        wide[buffer, row, :, chans:2 * chans] = normed.astype(jnp.bfloat16)
        wide[buffer, row, :, 2 * chans:] = after.astype(jnp.bfloat16)

    index = min(frame, mid.shape[0] - 1)
    for row in range(rows):
        stored = (top, mid, bot)[row // slab][index, row % slab]
        cells[row] = stored
        spread(row, stored, 0)

    base = 0
    for layer in range(depth):
        now = layer % 2
        count = rows - 2 * layer - 2
        waited = weights.at[layer] if first else weights.at[layer, 1]
        pltpu.make_async_copy(waited, waited, sems.at[layer]).wait()
        edges = [0, count] if count <= SPLIT else [0, count // 2, count]
        for low, high in zip(edges[:-1], edges[1:]):
            size = high - low
            start = layer + 1 + low
            total = earlier = None
            for tap in range(3):
                at = pl.ds(tap * 3 * chans, 3 * chans)
                block = wide[now, start - 1 + tap:start - 1 + tap + size].reshape(size * width, 3 * chans)
                here = jnp.dot(block, weights[layer, 1, at], preferred_element_type=jnp.float32)
                total = here if total is None else total + here
                if first:
                    there = jnp.dot(block, weights[layer, 0, at], preferred_element_type=jnp.float32)
                    earlier = there if earlier is None else earlier + there
            if first:
                older[base + low:base + high] = earlier.reshape(size, width, chans)
            for row in range(size):
                conv = total[row * width:(row + 1) * width]
                if not first:
                    conv = conv + older[base + low + row]
                place = start + row
                values = cells[place].astype(jnp.float32)
                stored = (values + conv / (1.0 + jnp.exp(-conv))).astype(jnp.bfloat16)
                cells[place] = stored
                if layer < depth - 1:
                    spread(place, stored, 1 - now)
                inner = place - slab
                if 0 <= inner < slab:
                    kept[core if inner < slab // 2 else other, layer, inner % (slab // 2)] = stored
                    if layer == depth - 1:
                        last[0, inner] = stored
        base += count


def run_frame(frame, meta, top, mid, bot, kernels, older=None):
    _, slab, width, chans = mid.shape
    taps = kernels[0].shape[0]
    vmem = pl.BlockSpec(memory_space=pltpu.VMEM)
    hbm = pl.BlockSpec(memory_space=pl.ANY)
    bf16 = jnp.bfloat16
    sums = DEPTH * (3 * slab - DEPTH - 1)
    out = [
        jax.ShapeDtypeStruct((2, DEPTH, slab // 2, width, chans), bf16),
        jax.ShapeDtypeStruct((1, slab, width, chans), bf16),
    ]
    extra = []
    if frame == 0:
        out.append(jax.ShapeDtypeStruct((sums, width, chans), jnp.float32))
    else:
        extra.append(older)
    work = 2 * sums * width * 9 * chans * chans * (2 - frame)
    return pl.pallas_call(
        functools.partial(frame_kernel, frame),
        out_shape=tuple(out),
        in_specs=[pl.BlockSpec(memory_space=pltpu.SMEM)] + [vmem] * 3 + [hbm] * len(kernels) + [vmem] * len(extra),
        out_specs=(vmem,) * len(out),
        scratch_shapes=[
            pltpu.VMEM((DEPTH, 2, taps, chans), bf16),
            pltpu.VMEM((3 * slab, width, chans), bf16),
            pltpu.VMEM((2, 3 * slab, width, 3 * chans), bf16),
            pltpu.SemaphoreType.DMA((DEPTH,)),
        ],
        compiler_params=pltpu.CompilerParams(vmem_limit_bytes=36 * 1024 * 1024),
        cost_estimate=pl.CostEstimate(flops=work, bytes_accessed=8 * 10**6, transcendentals=10**6),
        name="frame%d" % frame,
    )(meta, top, mid, bot, *kernels, *extra)


def place_kernel(meta, home, away, *refs):
    arrived, out = refs[:-1], refs[-1]
    x, core = meta[0], meta[1]
    out[2 * x + core] = home[...]
    out[2 * x + 1 - core] = away[...]
    for shift, pair in enumerate(arrived, 1):
        group = lax.rem(x - shift + 4, 4)
        out[2 * group + core] = pair[0]
        out[2 * group + 1 - core] = pair[1]


def place(meta, home, away, arrived):
    vmem = pl.BlockSpec(memory_space=pltpu.VMEM)
    return pl.pallas_call(
        place_kernel,
        out_shape=jax.ShapeDtypeStruct((8,) + home.shape, jnp.bfloat16),
        in_specs=[pl.BlockSpec(memory_space=pltpu.SMEM)] + [vmem] * (2 + len(arrived)),
        out_specs=vmem,
        compiler_params=pltpu.CompilerParams(vmem_limit_bytes=8 * 1024 * 1024),
        name="place",
    )(meta, home, away, *arrived)


def route(move, keep=lambda zh, x, zl, y, c: True):
    pairs = []
    for zh in range(2):
        for x in range(4):
            for zl in range(4):
                for y in range(8):
                    for c in range(2):
                        here = (zh, x, zl, y, c)
                        there = move(*here)
                        if there is not None and keep(*here):
                            pairs.append(tuple((((d[0] * 4 + d[1]) * 4 + d[2]) * 8 + d[3]) * 2 + d[4] for d in (here, there)))
    return pairs


def next_chip(step):
    def move(zh, x, zl, y, c):
        chip = zl * 8 + y + step
        return (zh, x, chip // 8, chip % 8, c) if 0 <= chip < 32 else None
    return move


def send(array, move, keep=lambda *here: True):
    return lax.ppermute(array, ("section", "rows"), route(move, keep))


def along_x(step):
    return lambda zh, x, zl, y, c: (zh, (x + step) % 4, zl, y, c)


def along_y(step):
    return lambda zh, x, zl, y, c: (zh, x, zl, (y + step) % 8, c)


def two_along_y(zh, x, zl, y, c):
    return (zh, x, zl, (y + (2 if y % 2 == 0 else -2)) % 8, c)


def hop(zh, x, zl, y, c):
    return (1, x, zl, y, c) if zh == 0 else None


def is_upper(zh, x, zl, y, c):
    return zh == 1


def sibling(zh, x, zl, y, c):
    return (zh, x, zl, y, 1 - c)


def local(frames_in, layer_weights):
    section, row = lax.axis_index("section"), lax.axis_index("rows")
    x, upper = section % 4, section // 4
    core, chip = row % 2, row // 2
    piece = chip % 4
    meta = jnp.stack([x, core, chip, piece, jnp.int32(32)]).astype(jnp.int32)
    chans = frames_in.shape[-1]

    own = layer_weights.reshape(2, 9 * chans, chans)
    part = own.shape[1] // 4
    quarter = lax.dynamic_slice(own, (core, piece * part, 0), (1, part, chans))[0]
    far = send(quarter, along_x(2))

    give = lax.dynamic_index_in_dim(frames_in, 2 * x + 1 - core, 0, keepdims=False)
    keep = lax.dynamic_index_in_dim(frames_in, 2 * x + core, 0, keepdims=False)
    got = send(give, sibling)
    mine = lax.dynamic_index_in_dim(own, core, 0, keepdims=False)
    theirs = lax.dynamic_index_in_dim(own, 1 - core, 0, keepdims=False)
    far, mine, got = lax.optimization_barrier((far, mine, got))
    left_mine = send(mine, along_x(1))
    right_mine = send(mine, along_x(-1))
    mid = jnp.where(core == 0, jnp.concatenate([keep, got], 1), jnp.concatenate([got, keep], 1))
    top = send(mid, next_chip(1))
    bot = send(mid, next_chip(-1))

    parts = (far, send(far, along_y(1)), send(far, along_y(-1)), send(far, two_along_y))
    *parts, top, bot = lax.optimization_barrier((*parts, top, bot))
    far_mine = jnp.stack(parts)
    far_theirs = send(far_mine, sibling)
    left_theirs = send(left_mine, sibling)
    right_theirs = send(right_mine, sibling)
    kernels = (mine, theirs, left_mine, left_theirs, right_mine, right_theirs, far_mine, far_theirs)

    kept, reached, older = run_frame(0, meta, top, mid, bot, kernels)
    mid_0 = send(reached, hop)
    first = [kept]
    kept, reached = run_frame(1, meta, top, mid, bot, kernels, older)
    first.append(kept)
    mid_1 = send(reached, hop)

    second = []
    top, bot = send(mid_0, next_chip(1), is_upper), send(mid_0, next_chip(-1), is_upper)
    kept, _, older = run_frame(0, meta, top, mid_0, bot, kernels)
    second.append(kept)
    top, bot = send(mid_1, next_chip(1), is_upper), send(mid_1, next_chip(-1), is_upper)
    kept, _ = run_frame(1, meta, top, mid_1, bot, kernels, older)
    second.append(kept)

    first, second = jnp.stack(first, 2), jnp.stack(second, 2)
    done = jnp.where(upper == 0, first, second)
    both = (done[0], send(done[1], sibling))
    home, away = [lax.dynamic_index_in_dim(one, x, 0, keepdims=False) for one in both]
    arrived = []
    for step in (1, 2, 3):
        layer = (x + step) % 4
        pair = jnp.stack([lax.dynamic_index_in_dim(one, layer, 0, keepdims=False) for one in both])
        arrived.append(send(pair, along_x(step)))
    return place(meta, home, away, arrived)[None]


def solution(mesh):
    placed = (P(None, None, "rows", None, None), P("section", None, None, None, None, None))
    return jax.shard_map(
        local,
        mesh=mesh,
        in_specs=placed,
        out_specs=P("section", None, None, "rows", None, None),
        check_vma=False,
    )
```

```python
import functools

import jax
import jax.numpy as jnp
from jax import lax
from jax.experimental import pallas as pl
from jax.experimental.pallas import tpu as pltpu
from jax.sharding import PartitionSpec as P

DEPTH = 4
SPLIT = 4


def frame_kernel(frame, meta, top, mid, bot, *refs):
    first = frame == 0
    refs = list(refs)
    pieces = refs[:8]
    older = refs[8]
    kept, last = (refs[9], refs[10]) if not first else (refs[8], refs[9])
    older = refs[8] if not first else refs[10]
    weights, cells, wide, sems, row_sem = refs[11:]
    x, core, chip, piece, chips = meta[0], meta[1], meta[2], meta[3], meta[4]
    depth, _, taps, chans = weights.shape
    _, slab, width, _ = mid.shape
    rows = 3 * slab
    other = 1 - core
    used = (0, 1) if first else (1,)

    index = min(frame, mid.shape[0] - 1)
    for place, source in enumerate((top, mid, bot)):
        pltpu.make_async_copy(source.at[index], cells.at[pl.ds(place * slab, slab)], row_sem).start()

    def fetch(layer, mine, theirs, places):
        for half in used:
            for source, owner in ((mine, core), (theirs, other)):
                @pl.when(owner == half)
                def _():
                    for at, block in places(source):
                        pltpu.make_async_copy(block, weights.at[layer, half, at], sems.at[layer]).start()

    def whole(source):
        return [(slice(None), source)]

    def quarters(source):
        part = taps // 4
        return [(pl.ds(pl.multiple_of(lax.rem(piece + shift, 4) * part, part), part), source.at[place])
                for place, shift in enumerate((0, 3, 1, 2))]

    for layer in range(depth):
        step = lax.rem(layer - x + depth, depth)
        for distance, at in ((0, 0), (1, 4), (3, 2), (2, 6)):
            @pl.when(step == distance)
            def _():
                fetch(layer, pieces[at], pieces[at + 1], quarters if distance == 2 else whole)

    column = lax.broadcasted_iota(jnp.int32, (width, chans), 0)

    def spread(row, stored, buffer):
        values = stored.astype(jnp.float32)
        place = chip * slab - slab + row
        inside = jnp.logical_and(place >= 0, place < chips * slab)
        scale = lax.rsqrt(jnp.mean(values * values, axis=-1, keepdims=True) + 1e-06)
        normed = values * jnp.where(inside, scale, 0.0)
        before = jnp.where(column == 0, 0.0, pltpu.roll(normed, 1, 0))
        after = jnp.where(column == width - 1, 0.0, pltpu.roll(normed, width - 1, 0))
        wide[buffer, row, :, 0:chans] = before.astype(jnp.bfloat16)
        wide[buffer, row, :, chans:2 * chans] = normed.astype(jnp.bfloat16)
        wide[buffer, row, :, 2 * chans:] = after.astype(jnp.bfloat16)

    pltpu.make_async_copy(cells, cells, row_sem).wait()
    for row in range(rows):
        spread(row, cells[row], 0)

    base = 0
    for layer in range(depth):
        now = layer % 2
        count = rows - 2 * layer - 2
        waited = weights.at[layer] if first else weights.at[layer, 1]
        pltpu.make_async_copy(waited, waited, sems.at[layer]).wait()
        edges = [0, count] if count <= SPLIT else [0, count // 2, count]
        for low, high in zip(edges[:-1], edges[1:]):
            size = high - low
            start = layer + 1 + low
            total = earlier = None
            for tap in range(3):
                at = pl.ds(tap * 3 * chans, 3 * chans)
                block = wide[now, start - 1 + tap:start - 1 + tap + size].reshape(size * width, 3 * chans)
                here = jnp.dot(block, weights[layer, 1, at], preferred_element_type=jnp.float32)
                total = here if total is None else total + here
                if first:
                    there = jnp.dot(block, weights[layer, 0, at], preferred_element_type=jnp.float32)
                    earlier = there if earlier is None else earlier + there
            if first:
                older[base + low:base + high] = earlier.reshape(size, width, chans)
            for row in range(size):
                conv = total[row * width:(row + 1) * width]
                if not first:
                    conv = conv + older[base + low + row]
                place = start + row
                values = cells[place].astype(jnp.float32)
                stored = (values + conv / (1.0 + jnp.exp(-conv))).astype(jnp.bfloat16)
                cells[place] = stored
                if layer < depth - 1:
                    spread(place, stored, 1 - now)
                inner = place - slab
                if 0 <= inner < slab:
                    kept[core if inner < slab // 2 else other, layer, inner % (slab // 2)] = stored
                    if layer == depth - 1:
                        last[0, inner] = stored
        base += count


def run_frame(frame, meta, top, mid, bot, kernels, older=None):
    _, slab, width, chans = mid.shape
    taps = kernels[0].shape[0]
    vmem = pl.BlockSpec(memory_space=pltpu.VMEM)
    hbm = pl.BlockSpec(memory_space=pl.ANY)
    bf16 = jnp.bfloat16
    sums = DEPTH * (3 * slab - DEPTH - 1)
    out = [
        jax.ShapeDtypeStruct((2, DEPTH, slab // 2, width, chans), bf16),
        jax.ShapeDtypeStruct((1, slab, width, chans), bf16),
    ]
    extra = []
    if frame == 0:
        out.append(jax.ShapeDtypeStruct((sums, width, chans), jnp.float32))
    else:
        extra.append(older)
    work = 2 * sums * width * 9 * chans * chans * (2 - frame)
    return pl.pallas_call(
        functools.partial(frame_kernel, frame),
        out_shape=tuple(out),
        in_specs=[pl.BlockSpec(memory_space=pltpu.SMEM)] + [hbm] * (3 + len(kernels)) + [vmem] * len(extra),
        out_specs=(vmem,) * len(out),
        scratch_shapes=[
            pltpu.VMEM((DEPTH, 2, taps, chans), bf16),
            pltpu.VMEM((3 * slab, width, chans), bf16),
            pltpu.VMEM((2, 3 * slab, width, 3 * chans), bf16),
            pltpu.SemaphoreType.DMA((DEPTH,)),
            pltpu.SemaphoreType.DMA,
        ],
        compiler_params=pltpu.CompilerParams(vmem_limit_bytes=50 * 1024 * 1024),
        cost_estimate=pl.CostEstimate(flops=work, bytes_accessed=8 * 10**6, transcendentals=10**6),
        name="frame%d" % frame,
    )(meta, top, mid, bot, *kernels, *extra)


def place_kernel(meta, home, away, *refs):
    arrived, out = refs[:-1], refs[-1]
    x, core = meta[0], meta[1]
    out[2 * x + core] = home[...]
    out[2 * x + 1 - core] = away[...]
    for shift, pair in enumerate(arrived, 1):
        group = lax.rem(x - shift + 4, 4)
        out[2 * group + core] = pair[0]
        out[2 * group + 1 - core] = pair[1]


def place(meta, home, away, arrived):
    vmem = pl.BlockSpec(memory_space=pltpu.VMEM)
    return pl.pallas_call(
        place_kernel,
        out_shape=jax.ShapeDtypeStruct((8,) + home.shape, jnp.bfloat16),
        in_specs=[pl.BlockSpec(memory_space=pltpu.SMEM)] + [vmem] * (2 + len(arrived)),
        out_specs=vmem,
        compiler_params=pltpu.CompilerParams(vmem_limit_bytes=8 * 1024 * 1024),
        name="place",
    )(meta, home, away, *arrived)


def route(move, keep=lambda zh, x, zl, y, c: True):
    pairs = []
    for zh in range(2):
        for x in range(4):
            for zl in range(4):
                for y in range(8):
                    for c in range(2):
                        here = (zh, x, zl, y, c)
                        there = move(*here)
                        if there is not None and keep(*here):
                            pairs.append(tuple((((d[0] * 4 + d[1]) * 4 + d[2]) * 8 + d[3]) * 2 + d[4] for d in (here, there)))
    return pairs


def next_chip(step):
    def move(zh, x, zl, y, c):
        chip = zl * 8 + y + step
        return (zh, x, chip // 8, chip % 8, c) if 0 <= chip < 32 else None
    return move


def send(array, move, keep=lambda *here: True):
    return lax.ppermute(array, ("section", "rows"), route(move, keep))


def along_x(step):
    return lambda zh, x, zl, y, c: (zh, (x + step) % 4, zl, y, c)


def along_y(step):
    return lambda zh, x, zl, y, c: (zh, x, zl, (y + step) % 8, c)


def two_along_y(zh, x, zl, y, c):
    return (zh, x, zl, (y + (2 if y % 2 == 0 else -2)) % 8, c)


def hop(zh, x, zl, y, c):
    return (1, x, zl, y, c) if zh == 0 else None


def is_upper(zh, x, zl, y, c):
    return zh == 1


def sibling(zh, x, zl, y, c):
    return (zh, x, zl, y, 1 - c)


def local(frames_in, layer_weights):
    section, row = lax.axis_index("section"), lax.axis_index("rows")
    x, upper = section % 4, section // 4
    core, chip = row % 2, row // 2
    piece = chip % 4
    meta = jnp.stack([x, core, chip, piece, jnp.int32(32)]).astype(jnp.int32)
    chans = frames_in.shape[-1]

    own = layer_weights.reshape(2, 9 * chans, chans)
    part = own.shape[1] // 4
    quarter = lax.dynamic_slice(own, (core, piece * part, 0), (1, part, chans))[0]
    far = send(quarter, along_x(2))

    give = lax.dynamic_index_in_dim(frames_in, 2 * x + 1 - core, 0, keepdims=False)
    give, quarter = lax.optimization_barrier((give, quarter))
    keep = lax.dynamic_index_in_dim(frames_in, 2 * x + core, 0, keepdims=False)
    got = send(give, sibling)
    mine = lax.dynamic_index_in_dim(own, core, 0, keepdims=False)
    theirs = lax.dynamic_index_in_dim(own, 1 - core, 0, keepdims=False)
    far, mine, got = lax.optimization_barrier((far, mine, got))
    left_mine = send(mine, along_x(1))
    right_mine = send(mine, along_x(-1))
    parts = (far, send(far, along_y(1)), send(far, along_y(-1)), send(far, two_along_y))
    got, early = lax.optimization_barrier((got, parts[2]))
    parts = (far, parts[1], early, parts[3])
    mid = jnp.where(core == 0, jnp.concatenate([keep, got], 1), jnp.concatenate([got, keep], 1))
    top = send(mid, next_chip(1))
    bot = send(mid, next_chip(-1))

    *parts, top, bot = lax.optimization_barrier((*parts, top, bot))
    far_mine = jnp.stack(parts)
    far_theirs = send(far_mine, sibling)
    left_theirs = send(left_mine, sibling)
    right_theirs = send(right_mine, sibling)
    kernels = (mine, theirs, left_mine, left_theirs, right_mine, right_theirs, far_mine, far_theirs)

    kept, reached, older = run_frame(0, meta, top, mid, bot, kernels)
    mid_0 = send(reached, hop)
    first = [kept]
    kept, reached = run_frame(1, meta, top, mid, bot, kernels, older)
    first.append(kept)
    mid_1 = send(reached, hop)

    second = []
    top, bot = send(mid_0, next_chip(1), is_upper), send(mid_0, next_chip(-1), is_upper)
    kept, _, older = run_frame(0, meta, top, mid_0, bot, kernels)
    second.append(kept)
    top, bot = send(mid_1, next_chip(1), is_upper), send(mid_1, next_chip(-1), is_upper)
    kept, _ = run_frame(1, meta, top, mid_1, bot, kernels, older)
    second.append(kept)

    first, second = jnp.stack(first, 2), jnp.stack(second, 2)
    done = jnp.where(upper == 0, first, second)
    both = (done[0], send(done[1], sibling))
    home, away = [lax.dynamic_index_in_dim(one, x, 0, keepdims=False) for one in both]
    arrived = []
    for step in (1, 2, 3):
        layer = (x + step) % 4
        pair = jnp.stack([lax.dynamic_index_in_dim(one, layer, 0, keepdims=False) for one in both])
        arrived.append(send(pair, along_x(step)))
    return place(meta, home, away, arrived)[None]


def solution(mesh):
    placed = (P(None, None, "rows", None, None), P("section", None, None, None, None, None))
    return jax.shard_map(
        local,
        mesh=mesh,
        in_specs=placed,
        out_specs=P("section", None, None, "rows", None, None),
        check_vma=False,
    )
```

```python
import functools

import jax
import jax.numpy as jnp
from jax import lax
from jax.experimental import pallas as pl
from jax.experimental.pallas import tpu as pltpu
from jax.sharding import PartitionSpec as P

DEPTH = 4
SPLIT = 4
LIMIT = 50


def frame_kernel(frame, builds, slabs, meta, *refs):
    first = frame == 0
    inputs, refs = refs[:slabs], list(refs[slabs:])
    fetches = inputs[0].shape[0] > 1
    if builds:
        pieces, refs = refs[:8], refs[8:]
    else:
        weights = refs.pop(0)
    older = refs.pop(0) if not first else None
    kept, last = refs.pop(0), refs.pop(0)
    older = refs.pop(0) if first else older
    if builds:
        weights = refs.pop(0)
    later = refs.pop(0) if fetches else None
    cells, wide, sems, row_sems = refs
    x, core, chip, piece, chips = meta[0], meta[1], meta[2], meta[3], meta[4]
    depth, _, taps, chans = weights.shape
    rows, width, _ = cells.shape
    slab = rows // 3
    other = 1 - core
    if fetches:
        for place, source in enumerate(inputs):
            at = pl.ds(place * slab, slab)
            pltpu.make_async_copy(source.at[0], cells.at[at], row_sems.at[0]).start()
            pltpu.make_async_copy(source.at[1], later.at[0, at], row_sems.at[1]).start()

    def fetch(layer, mine, theirs, places):
        for source, owner in ((mine, core), (theirs, other)):
            for at, block in places(source):
                pltpu.make_async_copy(block, weights.at[layer, owner, at], sems.at[layer]).start()

    def whole(source):
        return [(slice(None), source)]

    def quarters(source):
        part = taps // 4
        return [(pl.ds(pl.multiple_of(lax.rem(piece + shift, 4) * part, part), part), source.at[place])
                for place, shift in enumerate((0, 3, 1, 2))]

    if builds:
        for layer in range(depth):
            step = lax.rem(layer - x + depth, depth)
            for distance, at in ((0, 0), (1, 4), (3, 2), (2, 6)):
                @pl.when(step == distance)
                def _():
                    fetch(layer, pieces[at], pieces[at + 1], quarters if distance == 2 else whole)

    column = lax.broadcasted_iota(jnp.int32, (width, chans), 0)

    def spread(row, stored, buffer):
        values = stored.astype(jnp.float32)
        place = chip * slab - slab + row
        inside = jnp.logical_and(place >= 0, place < chips * slab)
        scale = lax.rsqrt(jnp.mean(values * values, axis=-1, keepdims=True) + 1e-06)
        normed = values * jnp.where(inside, scale, 0.0)
        before = jnp.where(column == 0, 0.0, pltpu.roll(normed, 1, 0))
        after = jnp.where(column == width - 1, 0.0, pltpu.roll(normed, width - 1, 0))
        wide[buffer, row, :, 0:chans] = before.astype(jnp.bfloat16)
        wide[buffer, row, :, chans:2 * chans] = normed.astype(jnp.bfloat16)
        wide[buffer, row, :, 2 * chans:] = after.astype(jnp.bfloat16)

    if fetches:
        pltpu.make_async_copy(cells, cells, row_sems.at[0]).wait()
    for row in range(rows):
        if fetches:
            stored = cells[row]
        else:
            depth_of = inputs[0].shape[1]
            stored = inputs[row // depth_of][0, row % depth_of]
            cells[row] = stored
        spread(row, stored, 0)

    base = 0
    for layer in range(depth):
        now = layer % 2
        count = rows - 2 * layer - 2
        if builds:
            pltpu.make_async_copy(weights.at[layer], weights.at[layer], sems.at[layer]).wait()
        edges = [0, count] if count <= SPLIT else [0, count // 2, count]
        for low, high in zip(edges[:-1], edges[1:]):
            size = high - low
            start = layer + 1 + low
            total = earlier = None
            for tap in range(3):
                at = pl.ds(tap * 3 * chans, 3 * chans)
                block = wide[now, start - 1 + tap:start - 1 + tap + size].reshape(size * width, 3 * chans)
                here = jnp.dot(block, weights[layer, 1, at], preferred_element_type=jnp.float32)
                total = here if total is None else total + here
                if first:
                    there = jnp.dot(block, weights[layer, 0, at], preferred_element_type=jnp.float32)
                    earlier = there if earlier is None else earlier + there
            if first:
                older[base + low:base + high] = earlier.reshape(size, width, chans)
            for row in range(size):
                conv = total[row * width:(row + 1) * width]
                if not first:
                    conv = conv + older[base + low + row]
                place = start + row
                values = cells[place].astype(jnp.float32)
                stored = (values + conv / (1.0 + jnp.exp(-conv))).astype(jnp.bfloat16)
                cells[place] = stored
                if layer < depth - 1:
                    spread(place, stored, 1 - now)
                inner = place - slab
                if 0 <= inner < slab:
                    kept[core if inner < slab // 2 else other, layer, inner % (slab // 2)] = stored
                    if layer == depth - 1:
                        last[0, inner] = stored
        base += count
    if fetches:
        pltpu.make_async_copy(later.at[0], later.at[0], row_sems.at[1]).wait()


def run_frame(frame, meta, inputs, kernels, older=None):
    _, _, width, chans = inputs[0].shape
    slab = sum(one.shape[1] for one in inputs) // 3
    fetches = inputs[0].shape[0] > 1
    builds = isinstance(kernels, tuple)
    if not builds:
        kernels = (kernels,)
    taps = kernels[0].shape[-2]
    vmem = pl.BlockSpec(memory_space=pltpu.VMEM)
    hbm = pl.BlockSpec(memory_space=pl.ANY)
    bf16 = jnp.bfloat16
    sums = DEPTH * (3 * slab - DEPTH - 1)
    gathered = jax.ShapeDtypeStruct((DEPTH, 2, taps, chans), bf16)
    out = [
        jax.ShapeDtypeStruct((2, DEPTH, slab // 2, width, chans), bf16),
        jax.ShapeDtypeStruct((1, slab, width, chans), bf16),
    ]
    extra = []
    if frame == 0:
        out.append(jax.ShapeDtypeStruct((sums, width, chans), jnp.float32))
    else:
        extra.append(older)
    if builds:
        out.append(gathered)
    if fetches:
        out.append(jax.ShapeDtypeStruct((1, 3 * slab, width, chans), bf16))
    work = 2 * sums * width * 9 * chans * chans * (2 - frame)
    return pl.pallas_call(
        functools.partial(frame_kernel, frame, builds, len(inputs)),
        out_shape=tuple(out),
        in_specs=[pl.BlockSpec(memory_space=pltpu.SMEM)]
        + [hbm if fetches else vmem] * len(inputs)
        + [hbm if builds else vmem] * len(kernels) + [vmem] * len(extra),
        out_specs=(vmem,) * len(out),
        scratch_shapes=[
            pltpu.VMEM((3 * slab, width, chans), bf16),
            pltpu.VMEM((2, 3 * slab, width, 3 * chans), bf16),
            pltpu.SemaphoreType.DMA((DEPTH,)),
            pltpu.SemaphoreType.DMA((2,)),
        ],
        compiler_params=pltpu.CompilerParams(vmem_limit_bytes=LIMIT * 1024 * 1024),
        cost_estimate=pl.CostEstimate(flops=work, bytes_accessed=8 * 10**6, transcendentals=10**6),
        name="frame%d" % frame,
    )(meta, *inputs, *kernels, *extra)


def place_kernel(meta, home, away, *refs):
    arrived, out = refs[:-1], refs[-1]
    x, core = meta[0], meta[1]
    out[2 * x + core] = home[...]
    out[2 * x + 1 - core] = away[...]
    for shift, pair in enumerate(arrived, 1):
        group = lax.rem(x - shift + 4, 4)
        out[2 * group + core] = pair[0]
        out[2 * group + 1 - core] = pair[1]


def place(meta, home, away, arrived):
    vmem = pl.BlockSpec(memory_space=pltpu.VMEM)
    return pl.pallas_call(
        place_kernel,
        out_shape=jax.ShapeDtypeStruct((8,) + home.shape, jnp.bfloat16),
        in_specs=[pl.BlockSpec(memory_space=pltpu.SMEM)] + [vmem] * (2 + len(arrived)),
        out_specs=vmem,
        compiler_params=pltpu.CompilerParams(vmem_limit_bytes=8 * 1024 * 1024),
        name="place",
    )(meta, home, away, *arrived)


def route(move, keep=lambda zh, x, zl, y, c: True):
    pairs = []
    for zh in range(2):
        for x in range(4):
            for zl in range(4):
                for y in range(8):
                    for c in range(2):
                        here = (zh, x, zl, y, c)
                        there = move(*here)
                        if there is not None and keep(*here):
                            pairs.append(tuple((((d[0] * 4 + d[1]) * 4 + d[2]) * 8 + d[3]) * 2 + d[4] for d in (here, there)))
    return pairs


def next_chip(step):
    def move(zh, x, zl, y, c):
        chip = zl * 8 + y + step
        return (zh, x, chip // 8, chip % 8, c) if 0 <= chip < 32 else None
    return move


def send(array, move, keep=lambda *here: True):
    return lax.ppermute(array, ("section", "rows"), route(move, keep))


def along_x(step):
    return lambda zh, x, zl, y, c: (zh, (x + step) % 4, zl, y, c)


def along_y(step):
    return lambda zh, x, zl, y, c: (zh, x, zl, (y + step) % 8, c)


def two_along_y(zh, x, zl, y, c):
    return (zh, x, zl, (y + (2 if y % 2 == 0 else -2)) % 8, c)


def hop(zh, x, zl, y, c):
    return (1, x, zl, y, c) if zh == 0 else None


def is_upper(zh, x, zl, y, c):
    return zh == 1


def sibling(zh, x, zl, y, c):
    return (zh, x, zl, y, 1 - c)


def local(frames_in, layer_weights):
    section, row = lax.axis_index("section"), lax.axis_index("rows")
    x, upper = section % 4, section // 4
    core, chip = row % 2, row // 2
    piece = chip % 4
    meta = jnp.stack([x, core, chip, piece, jnp.int32(32)]).astype(jnp.int32)
    chans = frames_in.shape[-1]

    own = layer_weights.reshape(2, 9 * chans, chans)
    part = own.shape[1] // 4
    quarter = lax.dynamic_slice(own, (core, piece * part, 0), (1, part, chans))[0]
    far = send(quarter, along_x(2))

    give = lax.dynamic_index_in_dim(frames_in, 2 * x + 1 - core, 0, keepdims=False)
    give, quarter = lax.optimization_barrier((give, quarter))
    keep = lax.dynamic_index_in_dim(frames_in, 2 * x + core, 0, keepdims=False)
    got = send(give, sibling)
    mine = lax.dynamic_index_in_dim(own, core, 0, keepdims=False)
    theirs = lax.dynamic_index_in_dim(own, 1 - core, 0, keepdims=False)
    far, mine, got = lax.optimization_barrier((far, mine, got))
    left_mine = send(mine, along_x(1))
    right_mine = send(mine, along_x(-1))
    parts = (far, send(far, along_y(1)), send(far, along_y(-1)), send(far, two_along_y))
    mid = jnp.where(core == 0, jnp.concatenate([keep, got], 1), jnp.concatenate([got, keep], 1))
    top = send(mid, next_chip(1))
    bot = send(mid, next_chip(-1))

    *parts, top, bot = lax.optimization_barrier((*parts, top, bot))
    far_mine = jnp.stack(parts)
    far_theirs = send(far_mine, sibling)
    left_theirs = send(left_mine, sibling)
    right_theirs = send(right_mine, sibling)
    kernels = (mine, theirs, left_mine, left_theirs, right_mine, right_theirs, far_mine, far_theirs)

    kept, reached, older, weights, later = run_frame(0, meta, (top, mid, bot), kernels)
    mid_0 = send(reached, hop)
    first = [kept]
    kept, reached = run_frame(1, meta, (later,), weights, older)
    first.append(kept)
    mid_1 = send(reached, hop)

    second = []
    top, bot = send(mid_0, next_chip(1), is_upper), send(mid_0, next_chip(-1), is_upper)
    kept, _, older, weights = run_frame(0, meta, (top, mid_0, bot), kernels)
    second.append(kept)
    top, bot = send(mid_1, next_chip(1), is_upper), send(mid_1, next_chip(-1), is_upper)
    kept, _ = run_frame(1, meta, (top, mid_1, bot), weights, older)
    second.append(kept)

    first, second = jnp.stack(first, 2), jnp.stack(second, 2)
    done = jnp.where(upper == 0, first, second)
    both = (done[0], send(done[1], sibling))
    home, away = [lax.dynamic_index_in_dim(one, x, 0, keepdims=False) for one in both]
    arrived = []
    for step in (1, 2, 3):
        layer = (x + step) % 4
        pair = jnp.stack([lax.dynamic_index_in_dim(one, layer, 0, keepdims=False) for one in both])
        arrived.append(send(pair, along_x(step)))
    return place(meta, home, away, arrived)[None]


def solution(mesh):
    placed = (P(None, None, "rows", None, None), P("section", None, None, None, None, None))
    return jax.shard_map(
        local,
        mesh=mesh,
        in_specs=placed,
        out_specs=P("section", None, None, "rows", None, None),
        check_vma=False,
    )
```

```python
import functools

import jax
import jax.numpy as jnp
from jax import lax
from jax.experimental import pallas as pl
from jax.experimental.pallas import tpu as pltpu
from jax.sharding import PartitionSpec as P

DEPTH = 4
SPLIT = 4
LIMIT = 24


def frame_kernel(frame, builds, slabs, meta, *refs):
    first = frame == 0
    inputs, refs = refs[:slabs], list(refs[slabs:])
    fetches = inputs[0].shape[0] > 1
    if builds:
        pieces, refs = refs[:8], refs[8:]
    else:
        weights = refs.pop(0)
    older = refs.pop(0) if not first else None
    kept, last = refs.pop(0), refs.pop(0)
    older = refs.pop(0) if first else older
    if builds:
        weights = refs.pop(0)
    later = refs.pop(0) if fetches else None
    cells, wide, sems, row_sems = refs
    x, core, chip, piece, chips = meta[0], meta[1], meta[2], meta[3], meta[4]
    depth, _, taps, chans = weights.shape
    rows, width, _ = cells.shape
    slab = rows // 3
    other = 1 - core
    if fetches:
        for place, source in enumerate(inputs):
            at = pl.ds(place * slab, slab)
            pltpu.make_async_copy(source.at[0], cells.at[at], row_sems.at[0]).start()
            pltpu.make_async_copy(source.at[1], later.at[0, at], row_sems.at[1]).start()

    def fetch(layer, mine, theirs, places):
        for source, owner in ((mine, core), (theirs, other)):
            for at, block in places(source):
                pltpu.make_async_copy(block, weights.at[layer, owner, at], sems.at[layer]).start()

    def whole(source):
        return [(slice(None), source)]

    def quarters(source):
        part = taps // 4
        return [(pl.ds(pl.multiple_of(lax.rem(piece + shift, 4) * part, part), part), source.at[place])
                for place, shift in enumerate((0, 3, 1, 2))]

    if builds:
        for layer in range(depth):
            step = lax.rem(layer - x + depth, depth)
            for distance, at in ((0, 0), (1, 4), (3, 2), (2, 6)):
                @pl.when(step == distance)
                def _():
                    fetch(layer, pieces[at], pieces[at + 1], quarters if distance == 2 else whole)

    column = lax.broadcasted_iota(jnp.int32, (width, chans), 0)

    def spread(row, stored, buffer):
        values = stored.astype(jnp.float32)
        place = chip * slab - slab + row
        inside = jnp.logical_and(place >= 0, place < chips * slab)
        scale = lax.rsqrt(jnp.mean(values * values, axis=-1, keepdims=True) + 1e-06)
        normed = values * jnp.where(inside, scale, 0.0)
        before = jnp.where(column == 0, 0.0, pltpu.roll(normed, 1, 0))
        after = jnp.where(column == width - 1, 0.0, pltpu.roll(normed, width - 1, 0))
        wide[buffer, row, :, 0:chans] = before.astype(jnp.bfloat16)
        wide[buffer, row, :, chans:2 * chans] = normed.astype(jnp.bfloat16)
        wide[buffer, row, :, 2 * chans:] = after.astype(jnp.bfloat16)

    if fetches:
        pltpu.make_async_copy(cells, cells, row_sems.at[0]).wait()
    for row in range(rows):
        if fetches:
            stored = cells[row]
        else:
            depth_of = inputs[0].shape[1]
            stored = inputs[row // depth_of][0, row % depth_of]
            cells[row] = stored
        spread(row, stored, 0)

    base = 0
    for layer in range(depth):
        now = layer % 2
        count = rows - 2 * layer - 2
        if builds:
            pltpu.make_async_copy(weights.at[layer], weights.at[layer], sems.at[layer]).wait()
        edges = [0, count] if count <= SPLIT else [0, count // 2, count]
        for low, high in zip(edges[:-1], edges[1:]):
            size = high - low
            start = layer + 1 + low
            total = earlier = None
            for tap in range(3):
                at = pl.ds(tap * 3 * chans, 3 * chans)
                block = wide[now, start - 1 + tap:start - 1 + tap + size].reshape(size * width, 3 * chans)
                here = jnp.dot(block, weights[layer, 1, at], preferred_element_type=jnp.float32)
                total = here if total is None else total + here
                if first:
                    there = jnp.dot(block, weights[layer, 0, at], preferred_element_type=jnp.float32)
                    earlier = there if earlier is None else earlier + there
            if first:
                older[base + low:base + high] = earlier.reshape(size, width, chans)
            for row in range(size):
                conv = total[row * width:(row + 1) * width]
                if not first:
                    conv = conv + older[base + low + row]
                place = start + row
                values = cells[place].astype(jnp.float32)
                stored = (values + conv / (1.0 + jnp.exp(-conv))).astype(jnp.bfloat16)
                cells[place] = stored
                if layer < depth - 1:
                    spread(place, stored, 1 - now)
                inner = place - slab
                if 0 <= inner < slab:
                    kept[core if inner < slab // 2 else other, layer, inner % (slab // 2)] = stored
                    if layer == depth - 1:
                        last[0, inner] = stored
        base += count
    if fetches:
        pltpu.make_async_copy(later.at[0], later.at[0], row_sems.at[1]).wait()


def run_frame(frame, meta, inputs, kernels, older=None):
    _, _, width, chans = inputs[0].shape
    slab = sum(one.shape[1] for one in inputs) // 3
    fetches = inputs[0].shape[0] > 1
    builds = isinstance(kernels, tuple)
    if not builds:
        kernels = (kernels,)
    taps = kernels[0].shape[-2]
    vmem = pl.BlockSpec(memory_space=pltpu.VMEM)
    hbm = pl.BlockSpec(memory_space=pl.ANY)
    bf16 = jnp.bfloat16
    sums = DEPTH * (3 * slab - DEPTH - 1)
    gathered = jax.ShapeDtypeStruct((DEPTH, 2, taps, chans), bf16)
    out = [
        jax.ShapeDtypeStruct((2, DEPTH, slab // 2, width, chans), bf16),
        jax.ShapeDtypeStruct((1, slab, width, chans), bf16),
    ]
    extra = []
    if frame == 0:
        out.append(jax.ShapeDtypeStruct((sums, width, chans), jnp.float32))
    else:
        extra.append(older)
    if builds:
        out.append(gathered)
    if fetches:
        out.append(jax.ShapeDtypeStruct((1, 3 * slab, width, chans), bf16))
    work = 2 * sums * width * 9 * chans * chans * (2 - frame)
    return pl.pallas_call(
        functools.partial(frame_kernel, frame, builds, len(inputs)),
        out_shape=tuple(out),
        in_specs=[pl.BlockSpec(memory_space=pltpu.SMEM)]
        + [hbm if fetches else vmem] * len(inputs)
        + [hbm if builds else vmem] * len(kernels) + [vmem] * len(extra),
        out_specs=(vmem,) * len(out),
        scratch_shapes=[
            pltpu.VMEM((3 * slab, width, chans), bf16),
            pltpu.VMEM((2, 3 * slab, width, 3 * chans), bf16),
            pltpu.SemaphoreType.DMA((DEPTH,)),
            pltpu.SemaphoreType.DMA((2,)),
        ],
        compiler_params=pltpu.CompilerParams(vmem_limit_bytes=LIMIT * 1024 * 1024),
        cost_estimate=pl.CostEstimate(flops=work, bytes_accessed=8 * 10**6, transcendentals=10**6),
        name="frame%d" % frame,
    )(meta, *inputs, *kernels, *extra)


def place_kernel(meta, home, away, *refs):
    arrived, out = refs[:-1], refs[-1]
    x, core = meta[0], meta[1]
    out[2 * x + core] = home[...]
    out[2 * x + 1 - core] = away[...]
    for shift, pair in enumerate(arrived, 1):
        group = lax.rem(x - shift + 4, 4)
        out[2 * group + core] = pair[0]
        out[2 * group + 1 - core] = pair[1]


def place(meta, home, away, arrived):
    vmem = pl.BlockSpec(memory_space=pltpu.VMEM)
    return pl.pallas_call(
        place_kernel,
        out_shape=jax.ShapeDtypeStruct((8,) + home.shape, jnp.bfloat16),
        in_specs=[pl.BlockSpec(memory_space=pltpu.SMEM)] + [vmem] * (2 + len(arrived)),
        out_specs=vmem,
        compiler_params=pltpu.CompilerParams(vmem_limit_bytes=8 * 1024 * 1024),
        name="place",
    )(meta, home, away, *arrived)


def route(move, keep=lambda zh, x, zl, y, c: True):
    pairs = []
    for zh in range(2):
        for x in range(4):
            for zl in range(4):
                for y in range(8):
                    for c in range(2):
                        here = (zh, x, zl, y, c)
                        there = move(*here)
                        if there is not None and keep(*here):
                            pairs.append(tuple((((d[0] * 4 + d[1]) * 4 + d[2]) * 8 + d[3]) * 2 + d[4] for d in (here, there)))
    return pairs


def next_chip(step):
    def move(zh, x, zl, y, c):
        chip = zl * 8 + y + step
        return (zh, x, chip // 8, chip % 8, c) if 0 <= chip < 32 else None
    return move


def send(array, move, keep=lambda *here: True):
    return lax.ppermute(array, ("section", "rows"), route(move, keep))


def along_x(step):
    return lambda zh, x, zl, y, c: (zh, (x + step) % 4, zl, y, c)


def along_y(step):
    return lambda zh, x, zl, y, c: (zh, x, zl, (y + step) % 8, c)


def two_along_y(zh, x, zl, y, c):
    return (zh, x, zl, (y + (2 if y % 2 == 0 else -2)) % 8, c)


def hop(zh, x, zl, y, c):
    return (1, x, zl, y, c) if zh == 0 else None


def is_upper(zh, x, zl, y, c):
    return zh == 1


def sibling(zh, x, zl, y, c):
    return (zh, x, zl, y, 1 - c)


def local(frames_in, layer_weights):
    section, row = lax.axis_index("section"), lax.axis_index("rows")
    x, upper = section % 4, section // 4
    core, chip = row % 2, row // 2
    piece = chip % 4
    meta = jnp.stack([x, core, chip, piece, jnp.int32(32)]).astype(jnp.int32)
    chans = frames_in.shape[-1]

    own = layer_weights.reshape(2, 9 * chans, chans)
    part = own.shape[1] // 4
    quarter = lax.dynamic_slice(own, (core, piece * part, 0), (1, part, chans))[0]
    far = send(quarter, along_x(2))

    give = lax.dynamic_index_in_dim(frames_in, 2 * x + 1 - core, 0, keepdims=False)
    keep = lax.dynamic_index_in_dim(frames_in, 2 * x + core, 0, keepdims=False)
    got = send(give, sibling)
    mine = lax.dynamic_index_in_dim(own, core, 0, keepdims=False)
    theirs = lax.dynamic_index_in_dim(own, 1 - core, 0, keepdims=False)
    mid = jnp.where(core == 0, jnp.concatenate([keep, got], 1), jnp.concatenate([got, keep], 1))
    top = send(mid, next_chip(1))
    bot = send(mid, next_chip(-1))

    far, mine, top, bot = lax.optimization_barrier((far, mine, top, bot))
    left_mine = send(mine, along_x(1))
    right_mine = send(mine, along_x(-1))
    parts = (far, send(far, along_y(1)), send(far, along_y(-1)), send(far, two_along_y))
    far_mine = jnp.stack(parts)
    far_theirs = send(far_mine, sibling)
    left_theirs = send(left_mine, sibling)
    right_theirs = send(right_mine, sibling)
    kernels = (mine, theirs, left_mine, left_theirs, right_mine, right_theirs, far_mine, far_theirs)

    rows = tuple(pltpu.with_memory_space_constraint(one, pltpu.HBM) for one in (top, mid, bot))
    kept, reached, older, weights, later = run_frame(0, meta, rows, kernels)
    mid_0 = send(reached, hop)
    first = [kept]
    kept, reached = run_frame(1, meta, (later,), weights, older)
    first.append(kept)
    mid_1 = send(reached, hop)

    second = []
    top, bot = send(mid_0, next_chip(1), is_upper), send(mid_0, next_chip(-1), is_upper)
    kept, _, older, weights = run_frame(0, meta, (top, mid_0, bot), kernels)
    second.append(kept)
    top, bot = send(mid_1, next_chip(1), is_upper), send(mid_1, next_chip(-1), is_upper)
    kept, _ = run_frame(1, meta, (top, mid_1, bot), weights, older)
    second.append(kept)

    first, second = jnp.stack(first, 2), jnp.stack(second, 2)
    done = jnp.where(upper == 0, first, second)
    both = (done[0], send(done[1], sibling))
    home, away = [lax.dynamic_index_in_dim(one, x, 0, keepdims=False) for one in both]
    arrived = []
    for step in (1, 2, 3):
        layer = (x + step) % 4
        pair = jnp.stack([lax.dynamic_index_in_dim(one, layer, 0, keepdims=False) for one in both])
        arrived.append(send(pair, along_x(step)))
    return place(meta, home, away, arrived)[None]


def solution(mesh):
    placed = (P(None, None, "rows", None, None), P("section", None, None, None, None, None))
    return jax.shard_map(
        local,
        mesh=mesh,
        in_specs=placed,
        out_specs=P("section", None, None, "rows", None, None),
        check_vma=False,
    )
```

```python
import functools

import jax
import jax.numpy as jnp
from jax import lax
from jax.experimental import pallas as pl
from jax.experimental.pallas import tpu as pltpu
from jax.sharding import PartitionSpec as P

DEPTH = 4
SPLIT = 4
LIMIT = 24


def fetch_weights(meta, pieces, weights, sems):
    x, core, piece = meta[0], meta[1], meta[3]
    depth, _, taps, _ = weights.shape
    part = taps // 4

    def whole(source):
        return [(slice(None), source)]

    def quarters(source):
        return [(pl.ds(pl.multiple_of(lax.rem(piece + shift, 4) * part, part), part), source.at[place])
                for place, shift in enumerate((0, 3, 1, 2))]

    for layer in range(depth):
        step = lax.rem(layer - x + depth, depth)
        for distance, at in ((0, 0), (1, 4), (3, 2), (2, 6)):
            @pl.when(step == distance)
            def _():
                for source, owner in ((pieces[at], core), (pieces[at + 1], 1 - core)):
                    for rows, block in (quarters if distance == 2 else whole)(source):
                        pltpu.make_async_copy(block, weights.at[layer, owner, rows], sems.at[layer]).start()


def gather_kernel(meta, *refs):
    pieces, weights, sems = refs[:8], refs[8], refs[9]
    fetch_weights(meta, pieces, weights, sems)
    for layer in range(DEPTH):
        pltpu.make_async_copy(weights.at[layer], weights.at[layer], sems.at[layer]).wait()


def gather(meta, kernels):
    taps, chans = kernels[0].shape
    return pl.pallas_call(
        gather_kernel,
        out_shape=jax.ShapeDtypeStruct((DEPTH, 2, taps, chans), jnp.bfloat16),
        in_specs=[pl.BlockSpec(memory_space=pltpu.SMEM)] + [pl.BlockSpec(memory_space=pl.ANY)] * 8,
        out_specs=pl.BlockSpec(memory_space=pltpu.VMEM),
        scratch_shapes=[pltpu.SemaphoreType.DMA((DEPTH,))],
        compiler_params=pltpu.CompilerParams(vmem_limit_bytes=LIMIT * 1024 * 1024),
        cost_estimate=pl.CostEstimate(flops=0, bytes_accessed=19 * 10**6, transcendentals=0),
        name="gather",
    )(meta, *kernels)


def frame_kernel(frame, builds, slabs, meta, *refs):
    first = frame == 0
    inputs, refs = refs[:slabs], list(refs[slabs:])
    fetches = inputs[0].shape[0] > 1
    if builds:
        pieces, refs = refs[:8], refs[8:]
    else:
        weights = refs.pop(0)
    older = refs.pop(0) if not first else None
    kept, last = refs.pop(0), refs.pop(0)
    older = refs.pop(0) if first else older
    if builds:
        weights = refs.pop(0)
    later = refs.pop(0) if fetches else None
    cells, wide, sems, row_sems = refs
    x, core, chip, piece, chips = meta[0], meta[1], meta[2], meta[3], meta[4]
    depth, _, taps, chans = weights.shape
    rows, width, _ = cells.shape
    slab = rows // 3
    other = 1 - core
    if fetches:
        for place, source in enumerate(inputs):
            at = pl.ds(place * slab, slab)
            pltpu.make_async_copy(source.at[0], cells.at[at], row_sems.at[0]).start()
            pltpu.make_async_copy(source.at[1], later.at[0, at], row_sems.at[1]).start()

    if builds:
        fetch_weights(meta, pieces, weights, sems)

    column = lax.broadcasted_iota(jnp.int32, (width, chans), 0)

    def spread(row, stored, buffer):
        values = stored.astype(jnp.float32)
        place = chip * slab - slab + row
        inside = jnp.logical_and(place >= 0, place < chips * slab)
        scale = lax.rsqrt(jnp.mean(values * values, axis=-1, keepdims=True) + 1e-06)
        normed = values * jnp.where(inside, scale, 0.0)
        before = jnp.where(column == 0, 0.0, pltpu.roll(normed, 1, 0))
        after = jnp.where(column == width - 1, 0.0, pltpu.roll(normed, width - 1, 0))
        wide[buffer, row, :, 0:chans] = before.astype(jnp.bfloat16)
        wide[buffer, row, :, chans:2 * chans] = normed.astype(jnp.bfloat16)
        wide[buffer, row, :, 2 * chans:] = after.astype(jnp.bfloat16)

    if fetches:
        pltpu.make_async_copy(cells, cells, row_sems.at[0]).wait()
    for row in range(rows):
        if fetches:
            stored = cells[row]
        else:
            depth_of = inputs[0].shape[1]
            stored = inputs[row // depth_of][0, row % depth_of]
            cells[row] = stored
        spread(row, stored, 0)

    base = 0
    for layer in range(depth):
        now = layer % 2
        count = rows - 2 * layer - 2
        if builds:
            pltpu.make_async_copy(weights.at[layer], weights.at[layer], sems.at[layer]).wait()
        edges = [0, count] if count <= SPLIT else [0, count // 2, count]
        for low, high in zip(edges[:-1], edges[1:]):
            size = high - low
            start = layer + 1 + low
            total = earlier = None
            for tap in range(3):
                at = pl.ds(tap * 3 * chans, 3 * chans)
                block = wide[now, start - 1 + tap:start - 1 + tap + size].reshape(size * width, 3 * chans)
                here = jnp.dot(block, weights[layer, 1, at], preferred_element_type=jnp.float32)
                total = here if total is None else total + here
                if first:
                    there = jnp.dot(block, weights[layer, 0, at], preferred_element_type=jnp.float32)
                    earlier = there if earlier is None else earlier + there
            if first:
                older[base + low:base + high] = earlier.reshape(size, width, chans)
            for row in range(size):
                conv = total[row * width:(row + 1) * width]
                if not first:
                    conv = conv + older[base + low + row]
                place = start + row
                values = cells[place].astype(jnp.float32)
                stored = (values + conv / (1.0 + jnp.exp(-conv))).astype(jnp.bfloat16)
                cells[place] = stored
                if layer < depth - 1:
                    spread(place, stored, 1 - now)
                inner = place - slab
                if 0 <= inner < slab:
                    kept[core if inner < slab // 2 else other, layer, inner % (slab // 2)] = stored
                    if layer == depth - 1:
                        last[0, inner] = stored
        base += count
    if fetches:
        pltpu.make_async_copy(later.at[0], later.at[0], row_sems.at[1]).wait()


def run_frame(frame, meta, inputs, kernels, older=None):
    _, _, width, chans = inputs[0].shape
    slab = sum(one.shape[1] for one in inputs) // 3
    fetches = inputs[0].shape[0] > 1
    builds = isinstance(kernels, tuple)
    if not builds:
        kernels = (kernels,)
    taps = kernels[0].shape[-2]
    vmem = pl.BlockSpec(memory_space=pltpu.VMEM)
    hbm = pl.BlockSpec(memory_space=pl.ANY)
    bf16 = jnp.bfloat16
    sums = DEPTH * (3 * slab - DEPTH - 1)
    gathered = jax.ShapeDtypeStruct((DEPTH, 2, taps, chans), bf16)
    out = [
        jax.ShapeDtypeStruct((2, DEPTH, slab // 2, width, chans), bf16),
        jax.ShapeDtypeStruct((1, slab, width, chans), bf16),
    ]
    extra = []
    if frame == 0:
        out.append(jax.ShapeDtypeStruct((sums, width, chans), jnp.float32))
    else:
        extra.append(older)
    if builds:
        out.append(gathered)
    if fetches:
        out.append(jax.ShapeDtypeStruct((1, 3 * slab, width, chans), bf16))
    work = 2 * sums * width * 9 * chans * chans * (2 - frame)
    return pl.pallas_call(
        functools.partial(frame_kernel, frame, builds, len(inputs)),
        out_shape=tuple(out),
        in_specs=[pl.BlockSpec(memory_space=pltpu.SMEM)]
        + [hbm if fetches else vmem] * len(inputs)
        + [hbm if builds else vmem] * len(kernels) + [vmem] * len(extra),
        out_specs=(vmem,) * len(out),
        scratch_shapes=[
            pltpu.VMEM((3 * slab, width, chans), bf16),
            pltpu.VMEM((2, 3 * slab, width, 3 * chans), bf16),
            pltpu.SemaphoreType.DMA((DEPTH,)),
            pltpu.SemaphoreType.DMA((2,)),
        ],
        compiler_params=pltpu.CompilerParams(vmem_limit_bytes=LIMIT * 1024 * 1024),
        cost_estimate=pl.CostEstimate(flops=work, bytes_accessed=8 * 10**6, transcendentals=10**6),
        name="frame%d" % frame,
    )(meta, *inputs, *kernels, *extra)


def place_kernel(meta, home, away, *refs):
    arrived, out = refs[:-1], refs[-1]
    x, core = meta[0], meta[1]
    out[2 * x + core] = home[...]
    out[2 * x + 1 - core] = away[...]
    for shift, pair in enumerate(arrived, 1):
        group = lax.rem(x - shift + 4, 4)
        out[2 * group + core] = pair[0]
        out[2 * group + 1 - core] = pair[1]


def place(meta, home, away, arrived):
    vmem = pl.BlockSpec(memory_space=pltpu.VMEM)
    return pl.pallas_call(
        place_kernel,
        out_shape=jax.ShapeDtypeStruct((8,) + home.shape, jnp.bfloat16),
        in_specs=[pl.BlockSpec(memory_space=pltpu.SMEM)] + [vmem] * (2 + len(arrived)),
        out_specs=vmem,
        compiler_params=pltpu.CompilerParams(vmem_limit_bytes=8 * 1024 * 1024),
        name="place",
    )(meta, home, away, *arrived)


def route(move, keep=lambda zh, x, zl, y, c: True):
    pairs = []
    for zh in range(2):
        for x in range(4):
            for zl in range(4):
                for y in range(8):
                    for c in range(2):
                        here = (zh, x, zl, y, c)
                        there = move(*here)
                        if there is not None and keep(*here):
                            pairs.append(tuple((((d[0] * 4 + d[1]) * 4 + d[2]) * 8 + d[3]) * 2 + d[4] for d in (here, there)))
    return pairs


def next_chip(step):
    def move(zh, x, zl, y, c):
        chip = zl * 8 + y + step
        return (zh, x, chip // 8, chip % 8, c) if 0 <= chip < 32 else None
    return move


def send(array, move, keep=lambda *here: True):
    return lax.ppermute(array, ("section", "rows"), route(move, keep))


def along_x(step):
    return lambda zh, x, zl, y, c: (zh, (x + step) % 4, zl, y, c)


def along_y(step):
    return lambda zh, x, zl, y, c: (zh, x, zl, (y + step) % 8, c)


def two_along_y(zh, x, zl, y, c):
    return (zh, x, zl, (y + (2 if y % 2 == 0 else -2)) % 8, c)


def hop(zh, x, zl, y, c):
    return (1, x, zl, y, c) if zh == 0 else None


def is_upper(zh, x, zl, y, c):
    return zh == 1


def sibling(zh, x, zl, y, c):
    return (zh, x, zl, y, 1 - c)


def local(frames_in, layer_weights):
    section, row = lax.axis_index("section"), lax.axis_index("rows")
    x, upper = section % 4, section // 4
    core, chip = row % 2, row // 2
    piece = chip % 4
    meta = jnp.stack([x, core, chip, piece, jnp.int32(32)]).astype(jnp.int32)
    chans = frames_in.shape[-1]

    own = layer_weights.reshape(2, 9 * chans, chans)
    part = own.shape[1] // 4
    quarter = lax.dynamic_slice(own, (core, piece * part, 0), (1, part, chans))[0]
    far = send(quarter, along_x(2))

    give = lax.dynamic_index_in_dim(frames_in, 2 * x + 1 - core, 0, keepdims=False)
    keep = lax.dynamic_index_in_dim(frames_in, 2 * x + core, 0, keepdims=False)
    got = send(give, sibling)
    mine = lax.dynamic_index_in_dim(own, core, 0, keepdims=False)
    theirs = lax.dynamic_index_in_dim(own, 1 - core, 0, keepdims=False)
    mid = jnp.where(core == 0, jnp.concatenate([keep, got], 1), jnp.concatenate([got, keep], 1))
    top = send(mid, next_chip(1))
    bot = send(mid, next_chip(-1))

    far, mine, bot = lax.optimization_barrier((far, mine, bot))
    left_mine = send(mine, along_x(1))
    right_mine = send(mine, along_x(-1))
    parts = (far, send(far, along_y(1)), send(far, along_y(-1)), send(far, two_along_y))
    *parts, top = lax.optimization_barrier((*parts, top))
    far_mine = jnp.stack(parts)
    far_theirs = send(far_mine, sibling)
    left_theirs = send(left_mine, sibling)
    right_theirs = send(right_mine, sibling)
    kernels = (mine, theirs, left_mine, left_theirs, right_mine, right_theirs, far_mine, far_theirs)

    rows = tuple(pltpu.with_memory_space_constraint(one, pltpu.HBM) for one in (top, mid, bot))
    kept, reached, older, weights, later = run_frame(0, meta, rows, kernels)
    mid_0 = send(reached, hop)
    first = [kept]
    kept, reached = run_frame(1, meta, (later,), weights, older)
    first.append(kept)
    mid_1 = send(reached, hop)

    later_meta, _ = lax.optimization_barrier((meta, mid_0))
    weights = gather(later_meta, kernels)
    mid_1, weights = lax.optimization_barrier((mid_1, weights))
    second = []
    top, bot = send(mid_0, next_chip(1), is_upper), send(mid_0, next_chip(-1), is_upper)
    kept, _, older = run_frame(0, meta, (top, mid_0, bot), weights)
    second.append(kept)
    top, bot = send(mid_1, next_chip(1), is_upper), send(mid_1, next_chip(-1), is_upper)
    kept, _ = run_frame(1, meta, (top, mid_1, bot), weights, older)
    second.append(kept)

    first, second = jnp.stack(first, 2), jnp.stack(second, 2)
    done = jnp.where(upper == 0, first, second)
    both = (done[0], send(done[1], sibling))
    home, away = [lax.dynamic_index_in_dim(one, x, 0, keepdims=False) for one in both]
    arrived = []
    for step in (1, 2, 3):
        layer = (x + step) % 4
        pair = jnp.stack([lax.dynamic_index_in_dim(one, layer, 0, keepdims=False) for one in both])
        arrived.append(send(pair, along_x(step)))
    return place(meta, home, away, arrived)[None]


def solution(mesh):
    placed = (P(None, None, "rows", None, None), P("section", None, None, None, None, None))
    return jax.shard_map(
        local,
        mesh=mesh,
        in_specs=placed,
        out_specs=P("section", None, None, "rows", None, None),
        check_vma=False,
    )
```

```python
import functools

import jax
import jax.numpy as jnp
from jax import lax
from jax.experimental import pallas as pl
from jax.experimental.pallas import tpu as pltpu
from jax.sharding import PartitionSpec as P

DEPTH = 4
SPLIT = 4
LIMIT = 24


def fetch_weights(meta, pieces, weights, sems):
    x, core, piece = meta[0], meta[1], meta[3]
    depth, _, taps, _ = weights.shape
    part = taps // 4

    def whole(source):
        return [(slice(None), source)]

    def quarters(source):
        return [(pl.ds(pl.multiple_of(lax.rem(piece + shift, 4) * part, part), part), source.at[place])
                for place, shift in enumerate((0, 3, 1, 2))]

    for layer in range(depth):
        step = lax.rem(layer - x + depth, depth)
        for distance, at in ((0, 0), (1, 4), (3, 2), (2, 6)):
            @pl.when(step == distance)
            def _():
                for source, owner in ((pieces[at], core), (pieces[at + 1], 1 - core)):
                    for rows, block in (quarters if distance == 2 else whole)(source):
                        pltpu.make_async_copy(block, weights.at[layer, owner, rows], sems.at[layer]).start()


def frame_kernel(frame, builds, slabs, meta, *refs):
    first = frame == 0
    inputs, refs = refs[:slabs], list(refs[slabs:])
    fetches = inputs[0].shape[0] > 1
    if builds:
        pieces, refs = refs[:8], refs[8:]
    else:
        weights = refs.pop(0)
    older = refs.pop(0) if not first else None
    kept, last = refs.pop(0), refs.pop(0)
    older = refs.pop(0) if first else older
    if builds:
        weights = refs.pop(0)
    later = refs.pop(0) if fetches else None
    cells, wide, sems, row_sems = refs
    x, core, chip, piece, chips = meta[0], meta[1], meta[2], meta[3], meta[4]
    depth, _, taps, chans = weights.shape
    rows, width, _ = cells.shape
    slab = rows // 3
    other = 1 - core
    if fetches:
        for place, source in enumerate(inputs):
            at = pl.ds(place * slab, slab)
            pltpu.make_async_copy(source.at[0], cells.at[at], row_sems.at[0]).start()
            pltpu.make_async_copy(source.at[1], later.at[0, at], row_sems.at[1]).start()

    if builds:
        fetch_weights(meta, pieces, weights, sems)

    column = lax.broadcasted_iota(jnp.int32, (width, chans), 0)

    def spread(row, stored, buffer):
        values = stored.astype(jnp.float32)
        place = chip * slab - slab + row
        inside = jnp.logical_and(place >= 0, place < chips * slab)
        scale = lax.rsqrt(jnp.mean(values * values, axis=-1, keepdims=True) + 1e-06)
        normed = values * jnp.where(inside, scale, 0.0)
        before = jnp.where(column == 0, 0.0, pltpu.roll(normed, 1, 0))
        after = jnp.where(column == width - 1, 0.0, pltpu.roll(normed, width - 1, 0))
        wide[buffer, row, :, 0:chans] = before.astype(jnp.bfloat16)
        wide[buffer, row, :, chans:2 * chans] = normed.astype(jnp.bfloat16)
        wide[buffer, row, :, 2 * chans:] = after.astype(jnp.bfloat16)

    if fetches:
        pltpu.make_async_copy(cells, cells, row_sems.at[0]).wait()
    for row in range(rows):
        if fetches:
            stored = cells[row]
        else:
            depth_of = inputs[0].shape[1]
            stored = inputs[row // depth_of][0, row % depth_of]
            cells[row] = stored
        spread(row, stored, 0)

    base = 0
    for layer in range(depth):
        now = layer % 2
        count = rows - 2 * layer - 2
        if builds:
            pltpu.make_async_copy(weights.at[layer], weights.at[layer], sems.at[layer]).wait()
        edges = [0, count] if count <= SPLIT else [0, count // 2, count]
        for low, high in zip(edges[:-1], edges[1:]):
            size = high - low
            start = layer + 1 + low
            total = earlier = None
            for tap in range(3):
                at = pl.ds(tap * 3 * chans, 3 * chans)
                block = wide[now, start - 1 + tap:start - 1 + tap + size].reshape(size * width, 3 * chans)
                here = jnp.dot(block, weights[layer, 1, at], preferred_element_type=jnp.float32)
                total = here if total is None else total + here
                if first:
                    there = jnp.dot(block, weights[layer, 0, at], preferred_element_type=jnp.float32)
                    earlier = there if earlier is None else earlier + there
            if first:
                older[base + low:base + high] = earlier.reshape(size, width, chans)
            for row in range(size):
                conv = total[row * width:(row + 1) * width]
                if not first:
                    conv = conv + older[base + low + row]
                place = start + row
                values = cells[place].astype(jnp.float32)
                stored = (values + conv / (1.0 + jnp.exp(-conv))).astype(jnp.bfloat16)
                cells[place] = stored
                if layer < depth - 1:
                    spread(place, stored, 1 - now)
                inner = place - slab
                if 0 <= inner < slab:
                    kept[core if inner < slab // 2 else other, layer, inner % (slab // 2)] = stored
                    if layer == depth - 1:
                        last[0, inner] = stored
        base += count
    if fetches:
        pltpu.make_async_copy(later.at[0], later.at[0], row_sems.at[1]).wait()


def run_frame(frame, meta, inputs, kernels, older=None):
    _, _, width, chans = inputs[0].shape
    slab = sum(one.shape[1] for one in inputs) // 3
    fetches = inputs[0].shape[0] > 1
    builds = isinstance(kernels, tuple)
    if not builds:
        kernels = (kernels,)
    taps = kernels[0].shape[-2]
    vmem = pl.BlockSpec(memory_space=pltpu.VMEM)
    hbm = pl.BlockSpec(memory_space=pl.ANY)
    bf16 = jnp.bfloat16
    sums = DEPTH * (3 * slab - DEPTH - 1)
    gathered = jax.ShapeDtypeStruct((DEPTH, 2, taps, chans), bf16)
    out = [
        jax.ShapeDtypeStruct((2, DEPTH, slab // 2, width, chans), bf16),
        jax.ShapeDtypeStruct((1, slab, width, chans), bf16),
    ]
    extra = []
    if frame == 0:
        out.append(jax.ShapeDtypeStruct((sums, width, chans), jnp.float32))
    else:
        extra.append(older)
    if builds:
        out.append(gathered)
    if fetches:
        out.append(jax.ShapeDtypeStruct((1, 3 * slab, width, chans), bf16))
    work = 2 * sums * width * 9 * chans * chans * (2 - frame)
    return pl.pallas_call(
        functools.partial(frame_kernel, frame, builds, len(inputs)),
        out_shape=tuple(out),
        in_specs=[pl.BlockSpec(memory_space=pltpu.SMEM)]
        + [hbm if fetches else vmem] * len(inputs)
        + [hbm if builds else vmem] * len(kernels) + [vmem] * len(extra),
        out_specs=(vmem,) * len(out),
        scratch_shapes=[
            pltpu.VMEM((3 * slab, width, chans), bf16),
            pltpu.VMEM((2, 3 * slab, width, 3 * chans), bf16),
            pltpu.SemaphoreType.DMA((DEPTH,)),
            pltpu.SemaphoreType.DMA((2,)),
        ],
        compiler_params=pltpu.CompilerParams(vmem_limit_bytes=LIMIT * 1024 * 1024),
        cost_estimate=pl.CostEstimate(flops=work, bytes_accessed=8 * 10**6, transcendentals=10**6),
        name="frame%d" % frame,
    )(meta, *inputs, *kernels, *extra)


def place_kernel(meta, home, away, *refs):
    arrived, out = refs[:-1], refs[-1]
    x, core = meta[0], meta[1]
    out[2 * x + core] = home[...]
    out[2 * x + 1 - core] = away[...]
    for shift, pair in enumerate(arrived, 1):
        group = lax.rem(x - shift + 4, 4)
        out[2 * group + core] = pair[0]
        out[2 * group + 1 - core] = pair[1]


def place(meta, home, away, arrived):
    vmem = pl.BlockSpec(memory_space=pltpu.VMEM)
    return pl.pallas_call(
        place_kernel,
        out_shape=jax.ShapeDtypeStruct((8,) + home.shape, jnp.bfloat16),
        in_specs=[pl.BlockSpec(memory_space=pltpu.SMEM)] + [vmem] * (2 + len(arrived)),
        out_specs=vmem,
        compiler_params=pltpu.CompilerParams(vmem_limit_bytes=8 * 1024 * 1024),
        name="place",
    )(meta, home, away, *arrived)


def route(move, keep=lambda zh, x, zl, y, c: True):
    pairs = []
    for zh in range(2):
        for x in range(4):
            for zl in range(4):
                for y in range(8):
                    for c in range(2):
                        here = (zh, x, zl, y, c)
                        there = move(*here)
                        if there is not None and keep(*here):
                            pairs.append(tuple((((d[0] * 4 + d[1]) * 4 + d[2]) * 8 + d[3]) * 2 + d[4] for d in (here, there)))
    return pairs


def next_chip(step):
    def move(zh, x, zl, y, c):
        chip = zl * 8 + y + step
        return (zh, x, chip // 8, chip % 8, c) if 0 <= chip < 32 else None
    return move


def send(array, move, keep=lambda *here: True):
    return lax.ppermute(array, ("section", "rows"), route(move, keep))


def along_x(step):
    return lambda zh, x, zl, y, c: (zh, (x + step) % 4, zl, y, c)


def along_y(step):
    return lambda zh, x, zl, y, c: (zh, x, zl, (y + step) % 8, c)


def two_along_y(zh, x, zl, y, c):
    return (zh, x, zl, (y + (2 if y % 2 == 0 else -2)) % 8, c)


def hop(zh, x, zl, y, c):
    return (1, x, zl, y, c) if zh == 0 else None


def is_upper(zh, x, zl, y, c):
    return zh == 1


def sibling(zh, x, zl, y, c):
    return (zh, x, zl, y, 1 - c)


def local(frames_in, layer_weights):
    section, row = lax.axis_index("section"), lax.axis_index("rows")
    x, upper = section % 4, section // 4
    core, chip = row % 2, row // 2
    piece = chip % 4
    meta = jnp.stack([x, core, chip, piece, jnp.int32(32)]).astype(jnp.int32)
    chans = frames_in.shape[-1]

    own = layer_weights.reshape(2, 9 * chans, chans)
    part = own.shape[1] // 4
    quarter = lax.dynamic_slice(own, (core, piece * part, 0), (1, part, chans))[0]
    far = send(quarter, along_x(2))

    give = lax.dynamic_index_in_dim(frames_in, 2 * x + 1 - core, 0, keepdims=False)
    keep = lax.dynamic_index_in_dim(frames_in, 2 * x + core, 0, keepdims=False)
    got = send(give, sibling)
    mine = lax.dynamic_index_in_dim(own, core, 0, keepdims=False)
    theirs = lax.dynamic_index_in_dim(own, 1 - core, 0, keepdims=False)
    mid = jnp.where(core == 0, jnp.concatenate([keep, got], 1), jnp.concatenate([got, keep], 1))
    bot = send(mid, next_chip(-1))

    far, mine, bot = lax.optimization_barrier((far, mine, bot))
    left_mine = send(mine, along_x(1))
    right_mine = send(mine, along_x(-1))
    parts = (far, send(far, along_y(1)), send(far, along_y(-1)), send(far, two_along_y))
    early, center = lax.optimization_barrier((parts[2], mid))
    top = send(center, next_chip(1))
    parts = (parts[0], parts[1], early, parts[3])
    *parts, top = lax.optimization_barrier((*parts, top))
    far_mine = jnp.stack(parts)
    far_theirs = send(far_mine, sibling)
    left_theirs = send(left_mine, sibling)
    right_theirs = send(right_mine, sibling)
    kernels = (mine, theirs, left_mine, left_theirs, right_mine, right_theirs, far_mine, far_theirs)

    rows = tuple(pltpu.with_memory_space_constraint(one, pltpu.HBM) for one in (top, mid, bot))
    kept, reached, older, weights, later = run_frame(0, meta, rows, kernels)
    mid_0 = send(reached, hop)
    first = [kept]
    kept, reached = run_frame(1, meta, (later,), weights, older)
    first.append(kept)
    mid_1 = send(reached, hop)

    second = []
    top, bot = send(mid_0, next_chip(1), is_upper), send(mid_0, next_chip(-1), is_upper)
    kept, _, older, weights = run_frame(0, meta, (top, mid_0, bot), kernels)
    second.append(kept)
    top, bot = send(mid_1, next_chip(1), is_upper), send(mid_1, next_chip(-1), is_upper)
    kept, _ = run_frame(1, meta, (top, mid_1, bot), weights, older)
    second.append(kept)

    first, second = jnp.stack(first, 2), jnp.stack(second, 2)
    done = jnp.where(upper == 0, first, second)
    both = (done[0], send(done[1], sibling))
    home, away = [lax.dynamic_index_in_dim(one, x, 0, keepdims=False) for one in both]
    arrived = []
    for step in (1, 2, 3):
        layer = (x + step) % 4
        pair = jnp.stack([lax.dynamic_index_in_dim(one, layer, 0, keepdims=False) for one in both])
        arrived.append(send(pair, along_x(step)))
    return place(meta, home, away, arrived)[None]


def solution(mesh):
    placed = (P(None, None, "rows", None, None), P("section", None, None, None, None, None))
    return jax.shard_map(
        local,
        mesh=mesh,
        in_specs=placed,
        out_specs=P("section", None, None, "rows", None, None),
        check_vma=False,
    )
```

```python
import functools

import jax
import jax.numpy as jnp
from jax import lax
from jax.experimental import pallas as pl
from jax.experimental.pallas import tpu as pltpu
from jax.sharding import PartitionSpec as P

DEPTH = 4
SPLIT = 4
LIMIT = 24
SHIFTS = (2, 1, 3)


def fetch_weights(meta, pieces, weights, sems):
    x, core, piece = meta[0], meta[1], meta[3]
    depth, _, taps, _ = weights.shape
    part = taps // 4

    def whole(source):
        return [(slice(None), source)]

    def quarters(source):
        return [(pl.ds(pl.multiple_of(lax.rem(piece + shift, 4) * part, part), part), source.at[place])
                for place, shift in enumerate((0, 3, 1, 2))]

    for layer in range(depth):
        step = lax.rem(layer - x + depth, depth)
        for distance, at in ((0, 0), (1, 4), (3, 2), (2, 6)):
            @pl.when(step == distance)
            def _():
                for source, owner in ((pieces[at], core), (pieces[at + 1], 1 - core)):
                    for rows, block in (quarters if distance == 2 else whole)(source):
                        pltpu.make_async_copy(block, weights.at[layer, owner, rows], sems.at[layer]).start()


def frame_kernel(frame, builds, slabs, meta, *refs):
    first = frame == 0
    inputs, refs = refs[:slabs], list(refs[slabs:])
    fetches = inputs[0].shape[0] > 1
    if builds:
        pieces, refs = refs[:8], refs[8:]
    else:
        weights = refs.pop(0)
    older = refs.pop(0) if not first else None
    kept, last = refs.pop(0), refs.pop(0)
    older = refs.pop(0) if first else older
    if builds:
        weights = refs.pop(0)
    later = refs.pop(0) if fetches else None
    cells, wide, sems, row_sems = refs
    x, core, chip, piece, chips = meta[0], meta[1], meta[2], meta[3], meta[4]
    depth, _, taps, chans = weights.shape
    rows, width, _ = cells.shape
    slab = rows // 3
    other = 1 - core
    if fetches:
        for place, source in enumerate(inputs):
            at = pl.ds(place * slab, slab)
            pltpu.make_async_copy(source.at[0], cells.at[at], row_sems.at[0]).start()
            pltpu.make_async_copy(source.at[1], later.at[0, at], row_sems.at[1]).start()

    if builds:
        fetch_weights(meta, pieces, weights, sems)

    column = lax.broadcasted_iota(jnp.int32, (width, chans), 0)

    def spread(row, stored, buffer):
        values = stored.astype(jnp.float32)
        place = chip * slab - slab + row
        inside = jnp.logical_and(place >= 0, place < chips * slab)
        scale = lax.rsqrt(jnp.mean(values * values, axis=-1, keepdims=True) + 1e-06)
        normed = values * jnp.where(inside, scale, 0.0)
        before = jnp.where(column == 0, 0.0, pltpu.roll(normed, 1, 0))
        after = jnp.where(column == width - 1, 0.0, pltpu.roll(normed, width - 1, 0))
        wide[buffer, row, :, 0:chans] = before.astype(jnp.bfloat16)
        wide[buffer, row, :, chans:2 * chans] = normed.astype(jnp.bfloat16)
        wide[buffer, row, :, 2 * chans:] = after.astype(jnp.bfloat16)

    if fetches:
        pltpu.make_async_copy(cells, cells, row_sems.at[0]).wait()
    for row in range(rows):
        if fetches:
            stored = cells[row]
        else:
            depth_of = inputs[0].shape[1]
            stored = inputs[row // depth_of][0, row % depth_of]
            cells[row] = stored
        spread(row, stored, 0)

    base = 0
    for layer in range(depth):
        now = layer % 2
        count = rows - 2 * layer - 2
        if builds:
            pltpu.make_async_copy(weights.at[layer], weights.at[layer], sems.at[layer]).wait()
        edges = [0, count] if count <= SPLIT else [0, count // 2, count]
        for low, high in zip(edges[:-1], edges[1:]):
            size = high - low
            start = layer + 1 + low
            total = earlier = None
            for tap in range(3):
                at = pl.ds(tap * 3 * chans, 3 * chans)
                block = wide[now, start - 1 + tap:start - 1 + tap + size].reshape(size * width, 3 * chans)
                here = jnp.dot(block, weights[layer, 1, at], preferred_element_type=jnp.float32)
                total = here if total is None else total + here
                if first:
                    there = jnp.dot(block, weights[layer, 0, at], preferred_element_type=jnp.float32)
                    earlier = there if earlier is None else earlier + there
            if first:
                older[base + low:base + high] = earlier.reshape(size, width, chans)
            for row in range(size):
                conv = total[row * width:(row + 1) * width]
                if not first:
                    conv = conv + older[base + low + row]
                place = start + row
                values = cells[place].astype(jnp.float32)
                stored = (values + conv / (1.0 + jnp.exp(-conv))).astype(jnp.bfloat16)
                cells[place] = stored
                if layer < depth - 1:
                    spread(place, stored, 1 - now)
                inner = place - slab
                if 0 <= inner < slab:
                    kept[core if inner < slab // 2 else other, layer, inner % (slab // 2)] = stored
                    if layer == depth - 1:
                        last[0, inner] = stored
        base += count
    if fetches:
        pltpu.make_async_copy(later.at[0], later.at[0], row_sems.at[1]).wait()


def run_frame(frame, meta, inputs, kernels, older=None):
    _, _, width, chans = inputs[0].shape
    slab = sum(one.shape[1] for one in inputs) // 3
    fetches = inputs[0].shape[0] > 1
    builds = isinstance(kernels, tuple)
    if not builds:
        kernels = (kernels,)
    taps = kernels[0].shape[-2]
    vmem = pl.BlockSpec(memory_space=pltpu.VMEM)
    hbm = pl.BlockSpec(memory_space=pl.ANY)
    bf16 = jnp.bfloat16
    sums = DEPTH * (3 * slab - DEPTH - 1)
    gathered = jax.ShapeDtypeStruct((DEPTH, 2, taps, chans), bf16)
    out = [
        jax.ShapeDtypeStruct((2, DEPTH, slab // 2, width, chans), bf16),
        jax.ShapeDtypeStruct((1, slab, width, chans), bf16),
    ]
    extra = []
    if frame == 0:
        out.append(jax.ShapeDtypeStruct((sums, width, chans), jnp.float32))
    else:
        extra.append(older)
    if builds:
        out.append(gathered)
    if fetches:
        out.append(jax.ShapeDtypeStruct((1, 3 * slab, width, chans), bf16))
    work = 2 * sums * width * 9 * chans * chans * (2 - frame)
    return pl.pallas_call(
        functools.partial(frame_kernel, frame, builds, len(inputs)),
        out_shape=tuple(out),
        in_specs=[pl.BlockSpec(memory_space=pltpu.SMEM)]
        + [hbm if fetches else vmem] * len(inputs)
        + [hbm if builds else vmem] * len(kernels) + [vmem] * len(extra),
        out_specs=(vmem,) * len(out),
        scratch_shapes=[
            pltpu.VMEM((3 * slab, width, chans), bf16),
            pltpu.VMEM((2, 3 * slab, width, 3 * chans), bf16),
            pltpu.SemaphoreType.DMA((DEPTH,)),
            pltpu.SemaphoreType.DMA((2,)),
        ],
        compiler_params=pltpu.CompilerParams(vmem_limit_bytes=LIMIT * 1024 * 1024),
        cost_estimate=pl.CostEstimate(flops=work, bytes_accessed=8 * 10**6, transcendentals=10**6),
        name="frame%d" % frame,
    )(meta, *inputs, *kernels, *extra)


def place_kernel(meta, home, away, *refs):
    arrived, out = refs[:-1], refs[-1]
    x, core = meta[0], meta[1]
    out[2 * x + core] = home[...]
    out[2 * x + 1 - core] = away[...]
    for shift, pair in zip(SHIFTS, arrived):
        group = lax.rem(x - shift + 4, 4)
        out[2 * group + core] = pair[0]
        out[2 * group + 1 - core] = pair[1]


def place(meta, home, away, arrived):
    vmem = pl.BlockSpec(memory_space=pltpu.VMEM)
    return pl.pallas_call(
        place_kernel,
        out_shape=jax.ShapeDtypeStruct((8,) + home.shape, jnp.bfloat16),
        in_specs=[pl.BlockSpec(memory_space=pltpu.SMEM)] + [vmem] * (2 + len(arrived)),
        out_specs=vmem,
        compiler_params=pltpu.CompilerParams(vmem_limit_bytes=8 * 1024 * 1024),
        name="place",
    )(meta, home, away, *arrived)


def route(move, keep=lambda zh, x, zl, y, c: True):
    pairs = []
    for zh in range(2):
        for x in range(4):
            for zl in range(4):
                for y in range(8):
                    for c in range(2):
                        here = (zh, x, zl, y, c)
                        there = move(*here)
                        if there is not None and keep(*here):
                            pairs.append(tuple((((d[0] * 4 + d[1]) * 4 + d[2]) * 8 + d[3]) * 2 + d[4] for d in (here, there)))
    return pairs


def next_chip(step):
    def move(zh, x, zl, y, c):
        chip = zl * 8 + y + step
        return (zh, x, chip // 8, chip % 8, c) if 0 <= chip < 32 else None
    return move


def send(array, move, keep=lambda *here: True):
    return lax.ppermute(array, ("section", "rows"), route(move, keep))


def along_x(step):
    return lambda zh, x, zl, y, c: (zh, (x + step) % 4, zl, y, c)


def along_y(step):
    return lambda zh, x, zl, y, c: (zh, x, zl, (y + step) % 8, c)


def two_along_y(zh, x, zl, y, c):
    return (zh, x, zl, (y + (2 if y % 2 == 0 else -2)) % 8, c)


def hop(zh, x, zl, y, c):
    return (1, x, zl, y, c) if zh == 0 else None


def is_upper(zh, x, zl, y, c):
    return zh == 1


def sibling(zh, x, zl, y, c):
    return (zh, x, zl, y, 1 - c)


def local(frames_in, layer_weights):
    section, row = lax.axis_index("section"), lax.axis_index("rows")
    x, upper = section % 4, section // 4
    core, chip = row % 2, row // 2
    piece = chip % 4
    meta = jnp.stack([x, core, chip, piece, jnp.int32(32)]).astype(jnp.int32)
    chans = frames_in.shape[-1]

    own = layer_weights.reshape(2, 9 * chans, chans)
    part = own.shape[1] // 4
    quarter = lax.dynamic_slice(own, (core, piece * part, 0), (1, part, chans))[0]
    far = send(quarter, along_x(2))

    give = lax.dynamic_index_in_dim(frames_in, 2 * x + 1 - core, 0, keepdims=False)
    keep = lax.dynamic_index_in_dim(frames_in, 2 * x + core, 0, keepdims=False)
    got = send(give, sibling)
    mine = lax.dynamic_index_in_dim(own, core, 0, keepdims=False)
    theirs = lax.dynamic_index_in_dim(own, 1 - core, 0, keepdims=False)
    mid = jnp.where(core == 0, jnp.concatenate([keep, got], 1), jnp.concatenate([got, keep], 1))
    bot = send(mid, next_chip(-1))

    far, mine, bot = lax.optimization_barrier((far, mine, bot))
    left_mine = send(mine, along_x(1))
    right_mine = send(mine, along_x(-1))
    parts = (far, send(far, along_y(1)), send(far, along_y(-1)), send(far, two_along_y))
    early, center = lax.optimization_barrier((parts[2], mid))
    top = send(center, next_chip(1))
    parts = (parts[0], parts[1], early, parts[3])
    far_mine = jnp.stack(parts)
    far_theirs = send(far_mine, sibling)
    left_theirs = send(left_mine, sibling)
    right_mine, top = lax.optimization_barrier((right_mine, top))
    right_theirs = send(right_mine, sibling)
    kernels = (mine, theirs, left_mine, left_theirs, right_mine, right_theirs, far_mine, far_theirs)

    rows = tuple(pltpu.with_memory_space_constraint(one, pltpu.HBM) for one in (top, mid, bot))
    kept, reached, older, weights, later = run_frame(0, meta, rows, kernels)
    mid_0 = send(reached, hop)
    first = [kept]
    kept, reached = run_frame(1, meta, (later,), weights, older)
    first.append(kept)
    mid_1 = send(reached, hop)

    second = []
    top, bot = send(mid_0, next_chip(1), is_upper), send(mid_0, next_chip(-1), is_upper)
    kept, _, older, weights = run_frame(0, meta, (top, mid_0, bot), kernels)
    second.append(kept)
    top, bot = send(mid_1, next_chip(1), is_upper), send(mid_1, next_chip(-1), is_upper)
    kept, _ = run_frame(1, meta, (top, mid_1, bot), weights, older)
    second.append(kept)

    first, second = jnp.stack(first, 2), jnp.stack(second, 2)
    done = jnp.where(upper == 0, first, second)
    both = (done[0], send(done[1], sibling))
    home, away = [lax.dynamic_index_in_dim(one, x, 0, keepdims=False) for one in both]
    arrived = []
    for step in SHIFTS:
        layer = (x + step) % 4
        pair = jnp.stack([lax.dynamic_index_in_dim(one, layer, 0, keepdims=False) for one in both])
        arrived.append(send(pair, along_x(step)))
    return place(meta, home, away, arrived)[None]


def solution(mesh):
    placed = (P(None, None, "rows", None, None), P("section", None, None, None, None, None))
    return jax.shard_map(
        local,
        mesh=mesh,
        in_specs=placed,
        out_specs=P("section", None, None, "rows", None, None),
        check_vma=False,
    )
```

```python
import functools

import jax
import jax.numpy as jnp
from jax import lax
from jax.experimental import pallas as pl
from jax.experimental.pallas import tpu as pltpu
from jax.sharding import PartitionSpec as P

DEPTH = 4
SPLIT = 2
LIMIT = 24
SHIFTS = (2, 1, 3)


def fetch_weights(meta, pieces, weights, sems):
    x, core, piece = meta[0], meta[1], meta[3]
    depth, _, taps, _ = weights.shape
    part = taps // 4

    def whole(source):
        return [(slice(None), source)]

    def quarters(source):
        return [(pl.ds(pl.multiple_of(lax.rem(piece + shift, 4) * part, part), part), source.at[place])
                for place, shift in enumerate((0, 3, 1, 2))]

    for layer in range(depth):
        step = lax.rem(layer - x + depth, depth)
        for distance, at in ((0, 0), (1, 4), (3, 2), (2, 6)):
            @pl.when(step == distance)
            def _():
                for source, owner in ((pieces[at], core), (pieces[at + 1], 1 - core)):
                    for rows, block in (quarters if distance == 2 else whole)(source):
                        pltpu.make_async_copy(block, weights.at[layer, owner, rows], sems.at[layer]).start()


def frame_kernel(frame, builds, slabs, meta, *refs):
    first = frame == 0
    inputs, refs = refs[:slabs], list(refs[slabs:])
    fetches = inputs[0].shape[0] > 1
    if builds:
        pieces, refs = refs[:8], refs[8:]
    else:
        weights = refs.pop(0)
    older = refs.pop(0) if not first else None
    kept, last = refs.pop(0), refs.pop(0)
    older = refs.pop(0) if first else older
    if builds:
        weights = refs.pop(0)
    later = refs.pop(0) if fetches else None
    cells, wide, sems, row_sems = refs
    x, core, chip, piece, chips = meta[0], meta[1], meta[2], meta[3], meta[4]
    depth, _, taps, chans = weights.shape
    rows, width, _ = cells.shape
    slab = rows // 3
    other = 1 - core
    if fetches:
        for place, source in enumerate(inputs):
            at = pl.ds(place * slab, slab)
            pltpu.make_async_copy(source.at[0], cells.at[at], row_sems.at[0]).start()
            pltpu.make_async_copy(source.at[1], later.at[0, at], row_sems.at[1]).start()

    if builds:
        fetch_weights(meta, pieces, weights, sems)

    column = lax.broadcasted_iota(jnp.int32, (width, chans), 0)

    def spread(row, stored, buffer):
        values = stored.astype(jnp.float32)
        place = chip * slab - slab + row
        inside = jnp.logical_and(place >= 0, place < chips * slab)
        scale = lax.rsqrt(jnp.mean(values * values, axis=-1, keepdims=True) + 1e-06)
        normed = values * jnp.where(inside, scale, 0.0)
        before = jnp.where(column == 0, 0.0, pltpu.roll(normed, 1, 0))
        after = jnp.where(column == width - 1, 0.0, pltpu.roll(normed, width - 1, 0))
        wide[buffer, row, :, 0:chans] = before.astype(jnp.bfloat16)
        wide[buffer, row, :, chans:2 * chans] = normed.astype(jnp.bfloat16)
        wide[buffer, row, :, 2 * chans:] = after.astype(jnp.bfloat16)

    if fetches:
        pltpu.make_async_copy(cells, cells, row_sems.at[0]).wait()
    for row in range(rows):
        if fetches:
            stored = cells[row]
        else:
            depth_of = inputs[0].shape[1]
            stored = inputs[row // depth_of][0, row % depth_of]
            cells[row] = stored
        spread(row, stored, 0)

    base = 0
    for layer in range(depth):
        now = layer % 2
        count = rows - 2 * layer - 2
        if builds:
            pltpu.make_async_copy(weights.at[layer], weights.at[layer], sems.at[layer]).wait()
        edges = [0, count] if count <= SPLIT else [0, count // 2, count]
        for low, high in zip(edges[:-1], edges[1:]):
            size = high - low
            start = layer + 1 + low
            total = earlier = None
            for tap in range(3):
                at = pl.ds(tap * 3 * chans, 3 * chans)
                block = wide[now, start - 1 + tap:start - 1 + tap + size].reshape(size * width, 3 * chans)
                here = jnp.dot(block, weights[layer, 1, at], preferred_element_type=jnp.float32)
                total = here if total is None else total + here
                if first:
                    there = jnp.dot(block, weights[layer, 0, at], preferred_element_type=jnp.float32)
                    earlier = there if earlier is None else earlier + there
            if first:
                older[base + low:base + high] = earlier.reshape(size, width, chans)
            for row in range(size):
                conv = total[row * width:(row + 1) * width]
                if not first:
                    conv = conv + older[base + low + row]
                place = start + row
                values = cells[place].astype(jnp.float32)
                stored = (values + conv / (1.0 + jnp.exp(-conv))).astype(jnp.bfloat16)
                cells[place] = stored
                if layer < depth - 1:
                    spread(place, stored, 1 - now)
                inner = place - slab
                if 0 <= inner < slab:
                    kept[core if inner < slab // 2 else other, layer, inner % (slab // 2)] = stored
                    if layer == depth - 1:
                        last[0, inner] = stored
        base += count
    if fetches:
        pltpu.make_async_copy(later.at[0], later.at[0], row_sems.at[1]).wait()


def run_frame(frame, meta, inputs, kernels, older=None):
    _, _, width, chans = inputs[0].shape
    slab = sum(one.shape[1] for one in inputs) // 3
    fetches = inputs[0].shape[0] > 1
    builds = isinstance(kernels, tuple)
    if not builds:
        kernels = (kernels,)
    taps = kernels[0].shape[-2]
    vmem = pl.BlockSpec(memory_space=pltpu.VMEM)
    hbm = pl.BlockSpec(memory_space=pl.ANY)
    bf16 = jnp.bfloat16
    sums = DEPTH * (3 * slab - DEPTH - 1)
    gathered = jax.ShapeDtypeStruct((DEPTH, 2, taps, chans), bf16)
    out = [
        jax.ShapeDtypeStruct((2, DEPTH, slab // 2, width, chans), bf16),
        jax.ShapeDtypeStruct((1, slab, width, chans), bf16),
    ]
    extra = []
    if frame == 0:
        out.append(jax.ShapeDtypeStruct((sums, width, chans), jnp.float32))
    else:
        extra.append(older)
    if builds:
        out.append(gathered)
    if fetches:
        out.append(jax.ShapeDtypeStruct((1, 3 * slab, width, chans), bf16))
    work = 2 * sums * width * 9 * chans * chans * (2 - frame)
    return pl.pallas_call(
        functools.partial(frame_kernel, frame, builds, len(inputs)),
        out_shape=tuple(out),
        in_specs=[pl.BlockSpec(memory_space=pltpu.SMEM)]
        + [hbm if fetches else vmem] * len(inputs)
        + [hbm if builds else vmem] * len(kernels) + [vmem] * len(extra),
        out_specs=(vmem,) * len(out),
        scratch_shapes=[
            pltpu.VMEM((3 * slab, width, chans), bf16),
            pltpu.VMEM((2, 3 * slab, width, 3 * chans), bf16),
            pltpu.SemaphoreType.DMA((DEPTH,)),
            pltpu.SemaphoreType.DMA((2,)),
        ],
        compiler_params=pltpu.CompilerParams(vmem_limit_bytes=LIMIT * 1024 * 1024),
        cost_estimate=pl.CostEstimate(flops=work, bytes_accessed=8 * 10**6, transcendentals=10**6),
        name="frame%d" % frame,
    )(meta, *inputs, *kernels, *extra)


def place_kernel(meta, home, away, *refs):
    arrived, out = refs[:-1], refs[-1]
    x, core = meta[0], meta[1]
    out[2 * x + core] = home[...]
    out[2 * x + 1 - core] = away[...]
    for shift, pair in zip(SHIFTS, arrived):
        group = lax.rem(x - shift + 4, 4)
        out[2 * group + core] = pair[0]
        out[2 * group + 1 - core] = pair[1]


def place(meta, home, away, arrived):
    vmem = pl.BlockSpec(memory_space=pltpu.VMEM)
    return pl.pallas_call(
        place_kernel,
        out_shape=jax.ShapeDtypeStruct((8,) + home.shape, jnp.bfloat16),
        in_specs=[pl.BlockSpec(memory_space=pltpu.SMEM)] + [vmem] * (2 + len(arrived)),
        out_specs=vmem,
        compiler_params=pltpu.CompilerParams(vmem_limit_bytes=8 * 1024 * 1024),
        name="place",
    )(meta, home, away, *arrived)


def route(move, keep=lambda zh, x, zl, y, c: True):
    pairs = []
    for zh in range(2):
        for x in range(4):
            for zl in range(4):
                for y in range(8):
                    for c in range(2):
                        here = (zh, x, zl, y, c)
                        there = move(*here)
                        if there is not None and keep(*here):
                            pairs.append(tuple((((d[0] * 4 + d[1]) * 4 + d[2]) * 8 + d[3]) * 2 + d[4] for d in (here, there)))
    return pairs


def next_chip(step):
    def move(zh, x, zl, y, c):
        chip = zl * 8 + y + step
        return (zh, x, chip // 8, chip % 8, c) if 0 <= chip < 32 else None
    return move


def send(array, move, keep=lambda *here: True):
    return lax.ppermute(array, ("section", "rows"), route(move, keep))


def along_x(step):
    return lambda zh, x, zl, y, c: (zh, (x + step) % 4, zl, y, c)


def along_y(step):
    return lambda zh, x, zl, y, c: (zh, x, zl, (y + step) % 8, c)


def two_along_y(zh, x, zl, y, c):
    return (zh, x, zl, (y + (2 if y % 2 == 0 else -2)) % 8, c)


def hop(zh, x, zl, y, c):
    return (1, x, zl, y, c) if zh == 0 else None


def is_upper(zh, x, zl, y, c):
    return zh == 1


def sibling(zh, x, zl, y, c):
    return (zh, x, zl, y, 1 - c)


def local(frames_in, layer_weights):
    section, row = lax.axis_index("section"), lax.axis_index("rows")
    x, upper = section % 4, section // 4
    core, chip = row % 2, row // 2
    piece = chip % 4
    meta = jnp.stack([x, core, chip, piece, jnp.int32(32)]).astype(jnp.int32)
    chans = frames_in.shape[-1]

    own = layer_weights.reshape(2, 9 * chans, chans)
    part = own.shape[1] // 4
    quarter = lax.dynamic_slice(own, (core, piece * part, 0), (1, part, chans))[0]
    far = send(quarter, along_x(2))

    give = lax.dynamic_index_in_dim(frames_in, 2 * x + 1 - core, 0, keepdims=False)
    keep = lax.dynamic_index_in_dim(frames_in, 2 * x + core, 0, keepdims=False)
    got = send(give, sibling)
    mine = lax.dynamic_index_in_dim(own, core, 0, keepdims=False)
    theirs = lax.dynamic_index_in_dim(own, 1 - core, 0, keepdims=False)
    mid = jnp.where(core == 0, jnp.concatenate([keep, got], 1), jnp.concatenate([got, keep], 1))
    bot = send(mid, next_chip(-1))

    far, mine, bot = lax.optimization_barrier((far, mine, bot))
    left_mine = send(mine, along_x(1))
    right_mine = send(mine, along_x(-1))
    parts = (far, send(far, along_y(1)), send(far, along_y(-1)), send(far, two_along_y))
    early, center = lax.optimization_barrier((parts[2], mid))
    top = send(center, next_chip(1))
    parts = (parts[0], parts[1], early, parts[3])
    far_mine = jnp.stack(parts)
    far_theirs = send(far_mine, sibling)
    left_theirs = send(left_mine, sibling)
    right_mine, top = lax.optimization_barrier((right_mine, top))
    right_theirs = send(right_mine, sibling)
    kernels = (mine, theirs, left_mine, left_theirs, right_mine, right_theirs, far_mine, far_theirs)

    rows = tuple(pltpu.with_memory_space_constraint(one, pltpu.HBM) for one in (top, mid, bot))
    kept, reached, older, weights, later = run_frame(0, meta, rows, kernels)
    mid_0 = send(reached, hop)
    first = [kept]
    kept, reached = run_frame(1, meta, (later,), weights, older)
    first.append(kept)
    mid_1 = send(reached, hop)

    second = []
    top, bot = send(mid_0, next_chip(1), is_upper), send(mid_0, next_chip(-1), is_upper)
    kept, _, older, weights = run_frame(0, meta, (top, mid_0, bot), kernels)
    second.append(kept)
    top, bot = send(mid_1, next_chip(1), is_upper), send(mid_1, next_chip(-1), is_upper)
    kept, _ = run_frame(1, meta, (top, mid_1, bot), weights, older)
    second.append(kept)

    first, second = jnp.stack(first, 2), jnp.stack(second, 2)
    done = jnp.where(upper == 0, first, second)
    both = (done[0], send(done[1], sibling))
    home, away = [lax.dynamic_index_in_dim(one, x, 0, keepdims=False) for one in both]
    arrived = []
    for step in SHIFTS:
        layer = (x + step) % 4
        pair = jnp.stack([lax.dynamic_index_in_dim(one, layer, 0, keepdims=False) for one in both])
        arrived.append(send(pair, along_x(step)))
    return place(meta, home, away, arrived)[None]


def solution(mesh):
    placed = (P(None, None, "rows", None, None), P("section", None, None, None, None, None))
    return jax.shard_map(
        local,
        mesh=mesh,
        in_specs=placed,
        out_specs=P("section", None, None, "rows", None, None),
        check_vma=False,
    )
```

```python
import functools

import jax
import jax.numpy as jnp
from jax import lax
from jax.experimental import pallas as pl
from jax.experimental.pallas import tpu as pltpu
from jax.sharding import PartitionSpec as P

DEPTH = 4
SPLIT = 2
LIMIT = 24
SHIFTS = (2, 1, 3)


def fetch_weights(meta, pieces, weights, sems):
    x, core, piece = meta[0], meta[1], meta[3]
    depth, _, taps, _ = weights.shape
    part = taps // 4

    def whole(source):
        return [(slice(None), source)]

    def quarters(source):
        return [(pl.ds(pl.multiple_of(lax.rem(piece + shift, 4) * part, part), part), source.at[place])
                for place, shift in enumerate((0, 3, 1, 2))]

    for layer in range(depth):
        step = lax.rem(layer - x + depth, depth)
        for distance, at in ((0, 0), (1, 4), (3, 2), (2, 6)):
            @pl.when(step == distance)
            def _():
                for source, owner in ((pieces[at], core), (pieces[at + 1], 1 - core)):
                    for rows, block in (quarters if distance == 2 else whole)(source):
                        pltpu.make_async_copy(block, weights.at[layer, owner, rows], sems.at[layer]).start()


def frame_kernel(frame, builds, slabs, meta, *refs):
    first = frame == 0
    inputs, refs = refs[:slabs], list(refs[slabs:])
    fetches = inputs[0].shape[0] > 1
    if builds:
        pieces, refs = refs[:8], refs[8:]
    else:
        weights = refs.pop(0)
    older = refs.pop(0) if not first else None
    kept, last = refs.pop(0), refs.pop(0)
    older = refs.pop(0) if first else older
    if builds:
        weights = refs.pop(0)
    later = refs.pop(0) if fetches else None
    cells, wide, sems, row_sems = refs
    x, core, chip, piece, chips = meta[0], meta[1], meta[2], meta[3], meta[4]
    depth, _, taps, chans = weights.shape
    rows, width, _ = cells.shape
    slab = rows // 3
    other = 1 - core
    if fetches:
        for place, source in enumerate(inputs):
            at = pl.ds(place * slab, slab)
            pltpu.make_async_copy(source.at[0], cells.at[at], row_sems.at[0]).start()
            pltpu.make_async_copy(source.at[1], later.at[0, at], row_sems.at[1]).start()

    if builds:
        fetch_weights(meta, pieces, weights, sems)

    column = lax.broadcasted_iota(jnp.int32, (width, chans), 0)

    def spread(row, stored, buffer):
        values = stored.astype(jnp.float32)
        place = chip * slab - slab + row
        inside = jnp.logical_and(place >= 0, place < chips * slab)
        scale = lax.rsqrt(jnp.mean(values * values, axis=-1, keepdims=True) + 1e-06)
        normed = values * jnp.where(inside, scale, 0.0)
        before = jnp.where(column == 0, 0.0, pltpu.roll(normed, 1, 0))
        after = jnp.where(column == width - 1, 0.0, pltpu.roll(normed, width - 1, 0))
        wide[buffer, row, :, 0:chans] = before.astype(jnp.bfloat16)
        wide[buffer, row, :, chans:2 * chans] = normed.astype(jnp.bfloat16)
        wide[buffer, row, :, 2 * chans:] = after.astype(jnp.bfloat16)

    if fetches:
        pltpu.make_async_copy(cells, cells, row_sems.at[0]).wait()
    for row in range(rows):
        if fetches:
            stored = cells[row]
        else:
            depth_of = inputs[0].shape[1]
            stored = inputs[row // depth_of][0, row % depth_of]
            cells[row] = stored
        spread(row, stored, 0)

    base = 0
    for layer in range(depth):
        now = layer % 2
        count = rows - 2 * layer - 2
        if builds:
            pltpu.make_async_copy(weights.at[layer], weights.at[layer], sems.at[layer]).wait()
        edges = [0, count] if count <= SPLIT else [0, count // 2, count]
        for low, high in zip(edges[:-1], edges[1:]):
            size = high - low
            start = layer + 1 + low
            total = earlier = None
            for tap in range(3):
                at = pl.ds(tap * 3 * chans, 3 * chans)
                block = wide[now, start - 1 + tap:start - 1 + tap + size].reshape(size * width, 3 * chans)
                here = jnp.dot(block, weights[layer, 1, at], preferred_element_type=jnp.float32)
                total = here if total is None else total + here
                if first:
                    there = jnp.dot(block, weights[layer, 0, at], preferred_element_type=jnp.float32)
                    earlier = there if earlier is None else earlier + there
            if first:
                older[base + low:base + high] = earlier.reshape(size, width, chans)
            for row in range(size):
                conv = total[row * width:(row + 1) * width]
                if not first:
                    conv = conv + older[base + low + row]
                place = start + row
                values = cells[place].astype(jnp.float32)
                stored = (values + conv / (1.0 + jnp.exp(-conv))).astype(jnp.bfloat16)
                cells[place] = stored
                if layer < depth - 1:
                    spread(place, stored, 1 - now)
                inner = place - slab
                if 0 <= inner < slab:
                    kept[core if inner < slab // 2 else other, layer, inner % (slab // 2)] = stored
                    if layer == depth - 1:
                        last[0, inner] = stored
        base += count
    if fetches:
        pltpu.make_async_copy(later.at[0], later.at[0], row_sems.at[1]).wait()


def run_frame(frame, meta, inputs, kernels, older=None):
    _, _, width, chans = inputs[0].shape
    slab = sum(one.shape[1] for one in inputs) // 3
    fetches = inputs[0].shape[0] > 1
    builds = isinstance(kernels, tuple)
    if not builds:
        kernels = (kernels,)
    taps = kernels[0].shape[-2]
    vmem = pl.BlockSpec(memory_space=pltpu.VMEM)
    hbm = pl.BlockSpec(memory_space=pl.ANY)
    bf16 = jnp.bfloat16
    sums = DEPTH * (3 * slab - DEPTH - 1)
    gathered = jax.ShapeDtypeStruct((DEPTH, 2, taps, chans), bf16)
    out = [
        jax.ShapeDtypeStruct((2, DEPTH, slab // 2, width, chans), bf16),
        jax.ShapeDtypeStruct((1, slab, width, chans), bf16),
    ]
    extra = []
    if frame == 0:
        out.append(jax.ShapeDtypeStruct((sums, width, chans), jnp.float32))
    else:
        extra.append(older)
    if builds:
        out.append(gathered)
    if fetches:
        out.append(jax.ShapeDtypeStruct((1, 3 * slab, width, chans), bf16))
    work = 2 * sums * width * 9 * chans * chans * (2 - frame)
    return pl.pallas_call(
        functools.partial(frame_kernel, frame, builds, len(inputs)),
        out_shape=tuple(out),
        in_specs=[pl.BlockSpec(memory_space=pltpu.SMEM)]
        + [hbm if fetches else vmem] * len(inputs)
        + [hbm if builds else vmem] * len(kernels) + [vmem] * len(extra),
        out_specs=(vmem,) * len(out),
        scratch_shapes=[
            pltpu.VMEM((3 * slab, width, chans), bf16),
            pltpu.VMEM((2, 3 * slab, width, 3 * chans), bf16),
            pltpu.SemaphoreType.DMA((DEPTH,)),
            pltpu.SemaphoreType.DMA((2,)),
        ],
        compiler_params=pltpu.CompilerParams(vmem_limit_bytes=LIMIT * 1024 * 1024),
        cost_estimate=pl.CostEstimate(flops=work, bytes_accessed=8 * 10**6, transcendentals=10**6),
        name="frame%d" % frame,
    )(meta, *inputs, *kernels, *extra)


def place_kernel(meta, home, away, *refs):
    arrived, out = refs[:-1], refs[-1]
    x, core = meta[0], meta[1]
    out[2 * x + core] = home[...]
    out[2 * x + 1 - core] = away[...]
    for shift, pair in zip(SHIFTS, arrived):
        group = lax.rem(x - shift + 4, 4)
        out[2 * group + core] = pair[0]
        out[2 * group + 1 - core] = pair[1]


def place(meta, home, away, arrived):
    vmem = pl.BlockSpec(memory_space=pltpu.VMEM)
    return pl.pallas_call(
        place_kernel,
        out_shape=jax.ShapeDtypeStruct((8,) + home.shape, jnp.bfloat16),
        in_specs=[pl.BlockSpec(memory_space=pltpu.SMEM)] + [vmem] * (2 + len(arrived)),
        out_specs=vmem,
        compiler_params=pltpu.CompilerParams(vmem_limit_bytes=8 * 1024 * 1024),
        name="place",
    )(meta, home, away, *arrived)


def route(move, keep=lambda zh, x, zl, y, c: True):
    pairs = []
    for zh in range(2):
        for x in range(4):
            for zl in range(4):
                for y in range(8):
                    for c in range(2):
                        here = (zh, x, zl, y, c)
                        there = move(*here)
                        if there is not None and keep(*here):
                            pairs.append(tuple((((d[0] * 4 + d[1]) * 4 + d[2]) * 8 + d[3]) * 2 + d[4] for d in (here, there)))
    return pairs


def next_chip(step):
    def move(zh, x, zl, y, c):
        chip = zl * 8 + y + step
        return (zh, x, chip // 8, chip % 8, c) if 0 <= chip < 32 else None
    return move


def send(array, move, keep=lambda *here: True):
    return lax.ppermute(array, ("section", "rows"), route(move, keep))


def along_x(step):
    return lambda zh, x, zl, y, c: (zh, (x + step) % 4, zl, y, c)


def along_y(step):
    return lambda zh, x, zl, y, c: (zh, x, zl, (y + step) % 8, c)


def two_along_y(zh, x, zl, y, c):
    return (zh, x, zl, (y + (2 if y % 2 == 0 else -2)) % 8, c)


def hop(zh, x, zl, y, c):
    return (1, x, zl, y, c) if zh == 0 else None


def is_upper(zh, x, zl, y, c):
    return zh == 1


def sibling(zh, x, zl, y, c):
    return (zh, x, zl, y, 1 - c)


def local(frames_in, layer_weights):
    section, row = lax.axis_index("section"), lax.axis_index("rows")
    x, upper = section % 4, section // 4
    core, chip = row % 2, row // 2
    piece = chip % 4
    meta = jnp.stack([x, core, chip, piece, jnp.int32(32)]).astype(jnp.int32)
    chans = frames_in.shape[-1]

    own = layer_weights.reshape(2, 9 * chans, chans)
    part = own.shape[1] // 4
    quarter = lax.dynamic_slice(own, (core, piece * part, 0), (1, part, chans))[0]
    give = lax.dynamic_index_in_dim(frames_in, 2 * x + 1 - core, 0, keepdims=False)
    keep = lax.dynamic_index_in_dim(frames_in, 2 * x + core, 0, keepdims=False)
    got = send(give, sibling)
    quarter, got = lax.optimization_barrier((quarter, got))
    far = send(quarter, along_x(2))
    mine = lax.dynamic_index_in_dim(own, core, 0, keepdims=False)
    theirs = lax.dynamic_index_in_dim(own, 1 - core, 0, keepdims=False)
    mid = jnp.where(core == 0, jnp.concatenate([keep, got], 1), jnp.concatenate([got, keep], 1))
    bot = send(mid, next_chip(-1))

    far, mine, bot = lax.optimization_barrier((far, mine, bot))
    left_mine = send(mine, along_x(1))
    right_mine = send(mine, along_x(-1))
    parts = (far, send(far, along_y(1)), send(far, along_y(-1)), send(far, two_along_y))
    early, center = lax.optimization_barrier((parts[2], mid))
    top = send(center, next_chip(1))
    parts = (parts[0], parts[1], early, parts[3])
    far_mine = jnp.stack(parts)
    far_theirs = send(far_mine, sibling)
    left_theirs = send(left_mine, sibling)
    right_mine, top = lax.optimization_barrier((right_mine, top))
    right_theirs = send(right_mine, sibling)
    kernels = (mine, theirs, left_mine, left_theirs, right_mine, right_theirs, far_mine, far_theirs)

    rows = tuple(pltpu.with_memory_space_constraint(one, pltpu.HBM) for one in (top, mid, bot))
    kept, reached, older, weights, later = run_frame(0, meta, rows, kernels)
    mid_0 = send(reached, hop)
    first = [kept]
    kept, reached = run_frame(1, meta, (later,), weights, older)
    first.append(kept)
    mid_1 = send(reached, hop)

    second = []
    top, bot = send(mid_0, next_chip(1), is_upper), send(mid_0, next_chip(-1), is_upper)
    kept, _, older, weights = run_frame(0, meta, (top, mid_0, bot), kernels)
    second.append(kept)
    top, bot = send(mid_1, next_chip(1), is_upper), send(mid_1, next_chip(-1), is_upper)
    kept, _ = run_frame(1, meta, (top, mid_1, bot), weights, older)
    second.append(kept)

    first, second = jnp.stack(first, 2), jnp.stack(second, 2)
    done = jnp.where(upper == 0, first, second)
    both = (done[0], send(done[1], sibling))
    home, away = [lax.dynamic_index_in_dim(one, x, 0, keepdims=False) for one in both]
    arrived = []
    for step in SHIFTS:
        layer = (x + step) % 4
        pair = jnp.stack([lax.dynamic_index_in_dim(one, layer, 0, keepdims=False) for one in both])
        arrived.append(send(pair, along_x(step)))
    return place(meta, home, away, arrived)[None]


def solution(mesh):
    placed = (P(None, None, "rows", None, None), P("section", None, None, None, None, None))
    return jax.shard_map(
        local,
        mesh=mesh,
        in_specs=placed,
        out_specs=P("section", None, None, "rows", None, None),
        check_vma=False,
    )
```
